256 devices in a mesh: grp: 4 (over x), leaf: 64 (over y, z, core).
Axes of the slice: x: 4, y: 4, z: 8, core: 2. Of those that a mesh axis runs over, the one named last changes fastest.
Arguments:
- basis: float32 [8, 524288], P(None, ('grp', 'leaf')), may hold values from -28 to 28
- roots: float32 [5], replicated, may hold values from 0.35 to 1
- near_blocks: bfloat16 [2048, 6, 256, 256], P(('grp', 'leaf')), may hold values from -0.046875 to 0.046875
- near_ids: int32 [2048, 6], P(('grp', 'leaf')), may hold values from 0 to 2047, as said below
- leaf_basis: bfloat16 [2048, 64, 256], P(('grp', 'leaf')), may hold values from -0.375 to 0.375
- far_coupling: bfloat16 [2048, 8, 64, 64], P(('grp', 'leaf')), may hold values from -0.109375 to 0.109375
- far_ids: int32 [2048, 8], P(('grp', 'leaf')), may hold values from 0 to 2047, as said below
- transfer: bfloat16 [2048, 64, 128], P(('grp', 'leaf')), may hold values from -0.5 to 0.5
- top_coupling: bfloat16 [1024, 8, 128, 128], P(('grp', 'leaf')), may hold values from -0.078125 to 0.078125
- top_ids: int32 [1024, 8], P(('grp', 'leaf')), may hold values from 0 to 1023, as said below
Outputs:
- next_vector: float32 [524288], P(('grp', 'leaf'))
- hessen: float32 [9], replicated
The draws below stay inside these ranges and needn't reach their ends.
Inputs may be any that keep to these rules, and one draw needn't show every extreme that they name: `near_ids`: row i starts with i itself; the others lie within 8 leaves of i. `far_ids`: every entry lies within 8 leaves of its row. `top_ids`: every entry lies within 4 parents of its row.
All inputs are finite; a program needn't handle non-finite values.
Results may differ from the reference program's by a relative error of at most 0.024.
Values may be sent and summed in bfloat16 or wider, within the bound.
No kernel may reach another device: no remote copies, remote signals or barrier semaphores. Data moves between devices by JAX's collectives and lax.ppermute only.
A program may use at most 64 MiB of HBM per device.

```python
import jax
import jax.numpy as jnp
from jax import lax

LEAF = 256
RANK = 64
PRANK = 128
LPD = 8
NEAR = 6
FAR = 8
TOPL = 8
BASIS = 8
ROOTS = 5
LEAVES = 2048
PARENTS = 1024
PANELS = 524288


def local_ids(key, rows_count, count, reach):
    rows = jnp.arange(rows_count, dtype=jnp.int32)[:, None]
    offsets = jax.random.randint(key, (rows_count, count), -reach, reach + 1)
    return jnp.clip(rows + offsets, 0, rows_count - 1).astype(jnp.int32)


def draw_near_ids(key, part):
    others = local_ids(jax.random.fold_in(key, 11), LEAVES, NEAR - 1, LPD)
    itself = jnp.arange(LEAVES, dtype=jnp.int32)[:, None]
    return jnp.concatenate([itself, others], axis=1).astype(jnp.int32)


def draw_far_ids(key, part):
    return local_ids(jax.random.fold_in(key, 23), LEAVES, FAR, LPD)


def draw_top_ids(key, part):
    return local_ids(jax.random.fold_in(key, 37), PARENTS, TOPL, LPD // 2)


def draw_basis(key, part):
    position = jnp.arange(PANELS, dtype=jnp.float32) / jnp.float32(PANELS)
    rising = jnp.exp2(2.0 * position)
    leaf_scale = jnp.exp(jax.random.uniform(jax.random.fold_in(key, 51), (LEAVES, 1), jnp.float32, jnp.log(0.7), jnp.log(1.4)))
    rough = jnp.broadcast_to(leaf_scale, (LEAVES, LEAF)).reshape(PANELS)
    noise = jnp.clip(jax.random.normal(jax.random.fold_in(key, 53), (BASIS, PANELS), jnp.float32), -4.0, 4.0)
    common = jnp.clip(jax.random.normal(jax.random.fold_in(key, 59), (1, PANELS), jnp.float32), -4.0, 4.0)
    values = noise + 0.4 * common
    return (values * (rising * rough)[None, :]).astype(jnp.float32)


def shard_levels(key, extent, split, low, largest):
    level, own = 1.0, jax.random.fold_in(key, 6)
    for dim, blocks in split:
        draws = jnp.exp(jax.random.uniform(jax.random.fold_in(own, dim), (blocks,), jnp.float32, low / len(split), largest / len(split)))
        level = level * jnp.repeat(draws, extent[dim] // blocks).reshape([-1 if axis == dim else 1 for axis in range(len(extent))])
    return level


def gaussian(rng, extent, scale, bound, split=(), kind=jnp.bfloat16):
    values = scale * jax.random.normal(rng, extent, jnp.float32)
    if split:
        values = values * shard_levels(rng, extent, split, -0.22, 0.18)
    return jnp.clip(values, -bound, bound).astype(kind)


def setup_inputs(seed: int = 0) -> dict:
    seeds = jax.random.split(jax.random.key(seed), 11)
    basis = draw_basis(jax.random.fold_in(seeds[10], 71), 0)
    roots = jnp.clip(jax.random.uniform(seeds[1], (ROOTS,), jnp.float32, 0.35, 1.0), 0.35, 1.0)
    near_blocks = gaussian(seeds[2], (LEAVES, NEAR, LEAF, LEAF), (LEAF * NEAR * 11) ** -0.5, 0.046875, ((0, 256),))
    near_ids = draw_near_ids(jax.random.fold_in(seeds[10], 71), 0)
    leaf_basis = gaussian(seeds[4], (LEAVES, RANK, LEAF), LEAF ** -0.5, 0.375, ((0, 256),))
    far_coupling = gaussian(seeds[5], (LEAVES, FAR, RANK, RANK), (FAR * RANK * 6) ** -0.5, 0.109375, ((0, 256),))
    far_ids = draw_far_ids(jax.random.fold_in(seeds[10], 71), 0)
    transfer = gaussian(seeds[7], (LEAVES, RANK, PRANK), (2 * RANK) ** -0.5, 0.5, ((0, 256),))
    top_coupling = gaussian(seeds[8], (PARENTS, TOPL, PRANK, PRANK), (TOPL * PRANK * 6) ** -0.5, 0.078125, ((0, 256),))
    top_ids = draw_top_ids(jax.random.fold_in(seeds[10], 71), 0)
    return dict(basis=basis, roots=roots, near_blocks=near_blocks, near_ids=near_ids, leaf_basis=leaf_basis, far_coupling=far_coupling, far_ids=far_ids, transfer=transfer, top_coupling=top_coupling, top_ids=top_ids)


def apply_operator(field, near_blocks, near_ids, leaf_basis, far_coupling, far_ids, transfer, top_coupling, top_ids):
    rounded = field.astype(jnp.bfloat16)
    groups = LEAVES // LPD

    def near_piece(pieces):
        blocks, indices = pieces
        nearby = rounded[indices].astype(jnp.float32)
        return jnp.einsum('lkab,lkb->la', blocks.astype(jnp.float32), nearby)
    near_term = lax.map(near_piece, (near_blocks.reshape(groups, LPD, NEAR, LEAF, LEAF), near_ids.reshape(groups, LPD, NEAR)))
    near_term = near_term.reshape(LEAVES, LEAF)
    coeffs = jnp.einsum('lra,la->lr', leaf_basis.astype(jnp.float32), rounded.astype(jnp.float32)).astype(jnp.bfloat16)
    partners = coeffs[far_ids].astype(jnp.float32)
    leaf_sum = jnp.einsum('lkrs,lks->lr', far_coupling.astype(jnp.float32), partners)
    upward = jnp.einsum('lrp,lr->lp', transfer.astype(jnp.float32), coeffs.astype(jnp.float32))
    upward = upward.reshape(PARENTS, 2, PRANK).sum(1).astype(jnp.bfloat16)
    sources = upward[top_ids].astype(jnp.float32)
    top_sum = jnp.einsum('pkab,pkb->pa', top_coupling.astype(jnp.float32), sources).astype(jnp.bfloat16)
    down = jnp.einsum('lrp,lp->lr', transfer.astype(jnp.float32), jnp.repeat(top_sum, 2, axis=0).astype(jnp.float32))
    local_coef = (leaf_sum + down).astype(jnp.bfloat16)
    far_term = jnp.einsum('lra,lr->la', leaf_basis.astype(jnp.float32), local_coef.astype(jnp.float32))
    return 0.5 * field + near_term + far_term

def reference(basis, roots, near_blocks, near_ids, leaf_basis, far_coupling, far_ids, transfer, top_coupling, top_ids):

    def operator(field):
        return apply_operator(field, near_blocks, near_ids, leaf_basis, far_coupling, far_ids, transfer, top_coupling, top_ids)
    vectors = basis.reshape(BASIS, LEAVES, LEAF)
    product = vectors[BASIS - 1]
    result = jnp.zeros_like(product)
    for index in range(ROOTS):
        result = result + product / roots[index]
        if index < ROOTS - 1:
            product = product - operator(product) / roots[index]
    image = operator(result)
    total = jnp.float32(PANELS)
    hcoef = jnp.einsum('mla,la->m', vectors, image, precision=lax.Precision.HIGHEST) / total
    remain = image - jnp.einsum('m,mla->la', hcoef, vectors, precision=lax.Precision.HIGHEST)
    beta = jnp.sqrt(jnp.sum(remain * remain) / total + 1e-06)
    next_vector = (remain / beta).reshape(PANELS)
    hessen = jnp.concatenate([hcoef, beta[None]])
    return (next_vector, hessen)
```

```python
import functools

import jax
import jax.numpy as jnp
from jax import lax
from jax.experimental import pallas as pl
from jax.experimental.pallas import tpu as pltpu
from jax.sharding import PartitionSpec as P

AXES = ("grp", "leaf")
F32 = jnp.float32
BF16 = jnp.bfloat16
NT = (((1,), (1,)), ((), ()))
VMEM = pl.BlockSpec(memory_space=pltpu.VMEM)
SMEM = pl.BlockSpec(memory_space=pltpu.SMEM)
PANEL, RANK, PRANK, WIDTH = 256, 64, 128, 512
T_AT, C_AT = PANEL, PANEL + PRANK


def write_stack(field, leaf_basis, transfer, stack):
    leaves = field.shape[0]
    rounded = field.astype(BF16)
    stack[...] = jnp.zeros(stack.shape, BF16)
    stack[:, :PANEL] = rounded
    coeffs = []
    for i in range(leaves):
        coeffs.append(
            lax.dot_general(rounded[i : i + 1], leaf_basis[i], NT, preferred_element_type=F32)
        )
    coeffs = jnp.concatenate(coeffs, axis=0).astype(BF16)
    stack[:, C_AT : C_AT + RANK] = coeffs
    parents = []
    for p in range(leaves // 2):
        total = jnp.zeros((1, PRANK), F32)
        for i in (2 * p, 2 * p + 1):
            total += jnp.dot(coeffs[i : i + 1], transfer[i], preferred_element_type=F32)
        parents.append(total)
    stack[: leaves // 2, T_AT : T_AT + PRANK] = jnp.concatenate(parents, axis=0).astype(BF16)


def fill_window(place, own, mate, far, window):
    leaves = own.shape[0]
    odd = place[0] % 2 == 1
    at = 0
    for part in window:
        lanes = slice(at, at + part.shape[1])
        at += part.shape[1]
        mate_v, far_v = mate[:, lanes].astype(F32), far[:, lanes].astype(F32)
        part[:leaves, :] = jnp.where(odd, mate_v, far_v)
        part[leaves : 2 * leaves, :] = own[:, lanes].astype(F32)
        part[2 * leaves :, :] = jnp.where(odd, far_v, mate_v)


def apply_rows(field, place, near_ids, far_ids, top_ids, near, leaf_basis, coupling, transfer, top, window):
    panel_win, parent_win, coeff_win = window
    leaves, parents = field.shape[0], field.shape[0] // 2
    first = place[0] * leaves - leaves
    first_parent = place[0] * parents - parents
    tops = []
    for p in range(parents):
        total = jnp.zeros((1, PRANK), F32)
        for k in range(top.shape[1]):
            q = top_ids[p, k] - first_parent
            row = (q // parents) * leaves + q % parents
            source = parent_win[pl.ds(row, 1), :].astype(BF16)
            total += lax.dot_general(source, top[p, k], NT, preferred_element_type=F32)
        tops.append(total.astype(BF16))
    rows = []
    for i in range(leaves):
        local = lax.dot_general(tops[i // 2], transfer[i], NT, preferred_element_type=F32)
        for k in range(coupling.shape[1]):
            source = coeff_win[pl.ds(far_ids[i, k] - first, 1), :][:, :RANK].astype(BF16)
            local += lax.dot_general(source, coupling[i, k], NT, preferred_element_type=F32)
        total = jnp.dot(local.astype(BF16), leaf_basis[i], preferred_element_type=F32)
        for k in range(near.shape[1]):
            source = panel_win[pl.ds(near_ids[i, k] - first, 1), :].astype(BF16)
            total += lax.dot_general(source, near[i, k], NT, preferred_element_type=F32)
        rows.append(total)
    return 0.5 * field + jnp.concatenate(rows, axis=0)


def start_kernel(basis, leaf_basis, transfer, product, stack):
    count, width = basis.shape[0], PANEL
    for i in range(product.shape[0]):
        product[i : i + 1, :] = basis[count - 1 : count, i * width : (i + 1) * width]
    write_stack(product[...], leaf_basis, transfer, stack)


def step_kernel(
    step, last, place, roots, near_ids, far_ids, top_ids, product, partial, own, mate, far,
    near, leaf_basis, coupling, transfer, top, product_out, partial_out, stack, *window,
):
    fill_window(place, own, mate, far, window)
    field = product[...]
    image = apply_rows(
        field, place, near_ids, far_ids, top_ids, near, leaf_basis, coupling, transfer, top, window
    )
    after = field - image / roots[step]
    total = partial[...] + field / roots[step]
    if last:
        total = total + after / roots[step + 1]
    product_out[...] = after
    partial_out[...] = total
    write_stack(total if last else after, leaf_basis, transfer, stack)


def last_kernel(
    place, near_ids, far_ids, top_ids, field, own, mate, far,
    near, leaf_basis, coupling, transfer, top, basis, image_out, sums, *window,
):
    fill_window(place, own, mate, far, window)
    image = apply_rows(
        field[...], place, near_ids, far_ids, top_ids, near, leaf_basis, coupling, transfer, top, window
    )
    image_out[...] = image
    count, leaves = basis.shape[0], image.shape[0]
    lane = lax.broadcasted_iota(jnp.int32, (count, 128), 1)
    sub = lax.broadcasted_iota(jnp.int32, (count, 128), 0)
    vectors = basis[...]
    packed = jnp.zeros((count, 128), F32)
    for n in range(count):
        column = jnp.sum(vectors * vectors[n : n + 1], axis=1, keepdims=True)
        packed = jnp.where(lane == n * count + sub, column, packed)
    dots = jnp.zeros((count, PANEL), F32)
    for i in range(leaves):
        dots += basis[:, i * PANEL : (i + 1) * PANEL] * image[i : i + 1]
    column = jnp.sum(dots, axis=1, keepdims=True)
    packed = jnp.where(lane == count * count + sub, column, packed)
    column = jnp.sum(image * image, axis=1, keepdims=True)
    packed = jnp.where(lane == count * count + count, column, packed)
    sums[...] = jnp.broadcast_to(jnp.sum(packed, axis=0, keepdims=True), sums.shape)


def finish_kernel(size, sums, image, basis, vector_out, hessen_out):
    count, leaves = basis.shape[0], image.shape[0]
    lane = lax.broadcasted_iota(jnp.int32, (count, 128), 1)
    sub = lax.broadcasted_iota(jnp.int32, (count, 128), 0)
    totals = jnp.broadcast_to(jnp.sum(sums[...], axis=0, keepdims=True) / size, (count, 128))
    zero = jnp.zeros((count, 128), F32)
    here = lane == count * count + sub
    coef = jnp.sum(jnp.where(here, totals, zero), axis=1, keepdims=True)
    inner = jnp.sum(jnp.where(lane % count == sub, coef, zero), axis=0, keepdims=True)
    outer = jnp.sum(jnp.where(lane // count == sub, coef, zero), axis=0, keepdims=True)
    gram = jnp.where(lane[:1] < count * count, totals[:1] * inner * outer, zero[:1])
    length = jnp.where(lane[:1] == count * count + count, totals[:1], zero[:1])
    squared = jnp.sum(gram + length, axis=1, keepdims=True)
    squared = squared - 2.0 * jnp.sum(coef * coef, axis=0, keepdims=True)
    beta = jnp.sqrt(squared + 1e-06)
    for i in range(leaves):
        taken = jnp.sum(coef * basis[:, i * PANEL : (i + 1) * PANEL], axis=0, keepdims=True)
        row = (image[i : i + 1, :] - taken) / beta
        vector_out[2 * i : 2 * i + 1, :] = row[:, : PANEL // 2]
        vector_out[2 * i + 1 : 2 * i + 2, :] = row[:, PANEL // 2 :]
    values = jnp.sum(jnp.where(lane == sub, coef, zero), axis=0, keepdims=True)
    hessen_out[...] = jnp.where(lane[:1] == count, beta, values)


def call(kernel, specs, outs, scratch=()):
    shapes = [jax.ShapeDtypeStruct(shape, dtype) for shape, dtype in outs]
    return pl.pallas_call(
        kernel,
        out_shape=shapes,
        in_specs=specs,
        out_specs=[VMEM] * len(shapes),
        scratch_shapes=list(scratch),
        compiler_params=pltpu.CompilerParams(vmem_limit_bytes=40 << 20),
    )


def body(
    basis, roots, near_blocks, near_ids, leaf_basis, far_coupling, far_ids, transfer, top_coupling, top_ids
):
    leaves = near_blocks.shape[0]
    devices = lax.axis_size("grp") * lax.axis_size("leaf")
    place = lax.axis_index(AXES).astype(jnp.int32).reshape(1)
    mates = [(i, i ^ 1) for i in range(devices)]
    others = [(i, ((i + 1) ^ 1) - 1) for i in range(devices)]
    others[0], others[-1] = (0, 0), (devices - 1, devices - 1)

    product, stack = call(
        start_kernel, [VMEM] * 3, [((leaves, PANEL), F32), ((leaves, WIDTH), BF16)]
    )(basis, leaf_basis, transfer)
    window = [pltpu.VMEM((3 * leaves, width), F32) for width in (PANEL, PRANK, WIDTH - C_AT)]
    matrices = (near_blocks, leaf_basis, far_coupling, transfer, top_coupling)
    partial = jnp.zeros((leaves, PANEL), F32)
    steps = roots.shape[0] - 1
    for step in range(steps):
        far = lax.ppermute(stack, AXES, others)
        mate = lax.ppermute(stack, AXES, mates)
        product, partial, stack = call(
            functools.partial(step_kernel, step, step == steps - 1),
            [SMEM] * 5 + [VMEM] * 10,
            [((leaves, PANEL), F32), ((leaves, PANEL), F32), ((leaves, WIDTH), BF16)],
            window,
        )(place, roots, near_ids, far_ids, top_ids, product, partial, stack, mate, far, *matrices)
    far = lax.ppermute(stack, AXES, others)
    mate = lax.ppermute(stack, AXES, mates)
    image, sums = call(
        last_kernel,
        [SMEM] * 4 + [VMEM] * 10,
        [((leaves, PANEL), F32), ((devices, 128), F32)],
        window,
    )(place, near_ids, far_ids, top_ids, partial, stack, mate, far, *matrices, basis)
    sums = lax.all_to_all(sums.reshape(devices, 1, 128), AXES, 0, 0, tiled=True)
    size = float(leaves * PANEL * devices)
    vector, hessen = call(
        functools.partial(finish_kernel, size), [VMEM] * 3, [((leaves * 2, 128), F32), ((1, 128), F32)]
    )(sums.reshape(devices, 128), image, basis)
    return vector.reshape(leaves * PANEL), hessen[0, : basis.shape[0] + 1]


def solution(mesh):
    split = P(AXES)
    in_specs = (P(None, AXES), P()) + (split,) * 8
    return jax.shard_map(body, mesh=mesh, in_specs=in_specs, out_specs=(split, P()), check_vma=False)
```

```python
import functools

import jax
import jax.numpy as jnp
from jax import lax
from jax.experimental import pallas as pl
from jax.experimental.pallas import tpu as pltpu
from jax.sharding import PartitionSpec as P

AXES = ("grp", "leaf")
F32 = jnp.float32
BF16 = jnp.bfloat16
NT = (((1,), (1,)), ((), ()))
VMEM = pl.BlockSpec(memory_space=pltpu.VMEM)
HBM = pl.BlockSpec(memory_space=pltpu.HBM)
PANEL, RANK, PRANK, WIDTH = 256, 64, 128, 512
T_AT, C_AT = PANEL, PANEL + PRANK
SOURCES = 32


def dot(a, b):
    return jnp.dot(a, b, preferred_element_type=F32)


def dot_nt(a, b):
    return lax.dot_general(a, b, NT, preferred_element_type=F32)


def diagonal(value, block):
    lane = lax.broadcasted_iota(jnp.int32, value.shape, 1)
    row = lax.broadcasted_iota(jnp.int32, value.shape, 0)
    return jnp.where(lane // block == row, value, jnp.zeros_like(value))


def flat(value):
    return jnp.broadcast_to(jnp.sum(value, axis=0, keepdims=True), value.shape)


def write_stack(field, leaf_basis, transfer, stack):
    rounded = field.astype(BF16)
    stack[:, :PANEL] = rounded
    kept = diagonal(dot_nt(rounded, leaf_basis), RANK)
    folded = sum(kept[:, at : at + 2 * RANK] for at in range(0, kept.shape[1], 2 * RANK))
    coeffs = folded[:, :RANK] + folded[:, RANK:]
    stack[:, C_AT:] = jnp.concatenate([coeffs, jnp.zeros_like(coeffs)], axis=1).astype(BF16)
    spread = diagonal(flat(kept.astype(BF16).astype(F32)), 2 * RANK)
    stack[:, T_AT:C_AT] = dot(spread.astype(BF16), transfer).astype(BF16)


def tiles(value, rows):
    return jnp.concatenate([value[at : at + rows] for at in range(0, value.shape[0], rows)], axis=1)


def apply_rows(field, own, mate, far, pick_near, pick_far, pick_top, near, leaf_basis, coupling, transfer, top):
    leaves = field.shape[0]
    rest = jnp.zeros((SOURCES - 3 * leaves, WIDTH), F32)
    window = jnp.concatenate(
        [own[...].astype(F32), mate[...].astype(F32), far[...].astype(F32), rest], axis=0
    ).astype(BF16)
    parents = tiles(dot(pick_top[...], window[:, T_AT:C_AT]), leaves).astype(BF16)
    coeffs = tiles(dot(pick_far[...], window[:, C_AT : C_AT + RANK]), leaves).astype(BF16)
    panels = dot(pick_near[...], window[:, :PANEL]).astype(BF16)
    tops = diagonal(dot(parents, top[...]), PRANK)
    tops = sum(tops[:, at : at + PRANK] for at in range(0, tops.shape[1], PRANK)).astype(BF16)
    local = diagonal(dot(coeffs, coupling[...]), RANK) + diagonal(dot_nt(tops, transfer), 2 * RANK)
    total = dot(diagonal(flat(local), RANK).astype(BF16), leaf_basis)
    row = lax.broadcasted_iota(jnp.int32, total.shape, 0)
    for i in range(leaves):
        image = jnp.zeros(total.shape, F32)
        for k in range(near.shape[1]):
            image += dot(panels[k * leaves : (k + 1) * leaves], near[i, k])
        total += jnp.where(row == i, image, jnp.zeros_like(image))
    return 0.5 * field + total


def stacked(ref):
    return ref[...].reshape(ref.shape[0] * ref.shape[1], ref.shape[2])


def start_kernel(basis, leaf_basis, transfer, product, stack, basis_in, leaf_basis_in, transfer_in, sems):
    copies = [
        pltpu.make_async_copy(source, target, sems.at[n])
        for n, (source, target) in enumerate(
            ((basis, basis_in), (leaf_basis, leaf_basis_in), (transfer, transfer_in))
        )
    ]
    for copy in copies:
        copy.start()
    for copy in copies:
        copy.wait()
    count = basis.shape[0]
    for i in range(product.shape[0]):
        product[i : i + 1, :] = basis_in[count - 1 : count, i * PANEL : (i + 1) * PANEL]
    write_stack(product[...], stacked(leaf_basis_in), stacked(transfer_in), stack)


def prepare_kernel(
    _, roots, near, near_ids, coupling, far_ids, top, top_ids,
    scales, near_out, coupling_out, top_out, pick_near, pick_far, pick_top,
    roots_in, near_in, coupling_in, top_in, near_ids_in, far_ids_in, top_ids_in, sems,
):
    leaves = near.shape[0]
    pairs = [
        (roots, roots_in), (near_ids, near_ids_in), (far_ids, far_ids_in), (top_ids, top_ids_in),
        (coupling, coupling_in), (top, top_in),
    ] + [(near.at[i], near_in.at[i]) for i in range(leaves)]
    copies = [
        pltpu.make_async_copy(source, target, sems.at[n]) for n, (source, target) in enumerate(pairs)
    ]
    for copy in copies:
        copy.start()
    for copy in copies[:4]:
        copy.wait()
    for k in range(roots.shape[1]):
        scales[k * leaves : (k + 1) * leaves, :] = jnp.broadcast_to(
            roots_in[:, k : k + 1], (leaves, scales.shape[1])
        )
    place = lax.axis_index(AXES)
    odd = place % 2 == 1
    left, right = jnp.where(odd, leaves, 2 * leaves), jnp.where(odd, 2 * leaves, leaves)
    for ids_in, pick, rows in (
        (near_ids_in, pick_near, leaves), (far_ids_in, pick_far, leaves), (top_ids_in, pick_top, leaves // 2),
    ):
        away = ids_in[...] - place * rows
        where = jnp.where(away < 0, away + rows + left, jnp.where(away < rows, away, away - rows + right))
        lane = lax.broadcasted_iota(jnp.int32, (rows, SOURCES), 1)
        for k in range(ids_in.shape[1]):
            hot = jnp.where(lane == where[:, k : k + 1], 1.0, 0.0)
            if rows < leaves:
                hot = jnp.concatenate([hot, jnp.zeros((leaves - rows, SOURCES), F32)], axis=0)
            pick[k * leaves : (k + 1) * leaves, :] = hot.astype(BF16)
    copies[4].wait()
    for i in range(leaves):
        for k in range(coupling.shape[1]):
            rows, lanes = slice(k * RANK, (k + 1) * RANK), slice(i * RANK, (i + 1) * RANK)
            coupling_out[rows, lanes] = coupling_in[i, k].T
    copies[5].wait()
    for p in range(top.shape[0]):
        for k in range(top.shape[1]):
            rows, lanes = slice(k * PRANK, (k + 1) * PRANK), slice(p * PRANK, (p + 1) * PRANK)
            top_out[rows, lanes] = top_in[p, k].T
    for i in range(leaves):
        copies[6 + i].wait()
        for k in range(near.shape[1]):
            near_out[i, k] = near_in[i, k].T


def step_kernel(
    step, last, scales, product, partial, own, mate, far, pick_near, pick_far, pick_top,
    near, leaf_basis, coupling, transfer, top, product_out, partial_out, stack,
):
    leaves = product.shape[0]
    basis_rows, transfer_rows = stacked(leaf_basis), stacked(transfer)
    field = product[...]
    image = apply_rows(
        field, own, mate, far, pick_near, pick_far, pick_top, near, basis_rows, coupling, transfer_rows, top
    )
    root = scales[step * leaves : (step + 1) * leaves, :]
    after = field - image / root
    total = field / root
    if step:
        total += partial[...]
    if last:
        total += after / scales[(step + 1) * leaves : (step + 2) * leaves, :]
    product_out[...] = after
    partial_out[...] = total
    write_stack(total if last else after, basis_rows, transfer_rows, stack)


def last_kernel(
    field, own, mate, far, pick_near, pick_far, pick_top,
    near, leaf_basis, coupling, transfer, top, basis, image_out, sums,
):
    image = apply_rows(
        field[...], own, mate, far, pick_near, pick_far, pick_top,
        near, stacked(leaf_basis), coupling, stacked(transfer), top,
    )
    image_out[...] = image
    count, leaves = basis.shape[0], image.shape[0]
    lane = lax.broadcasted_iota(jnp.int32, (count, 128), 1)
    sub = lax.broadcasted_iota(jnp.int32, (count, 128), 0)
    vectors = basis[...]
    packed = jnp.zeros((count, 128), F32)
    for n in range(count):
        column = jnp.sum(vectors * vectors[n : n + 1], axis=1, keepdims=True)
        packed = jnp.where(lane == n * count + sub, column, packed)
    dots = jnp.zeros((count, PANEL), F32)
    for i in range(leaves):
        dots += basis[:, i * PANEL : (i + 1) * PANEL] * image[i : i + 1]
    column = jnp.sum(dots, axis=1, keepdims=True)
    packed = jnp.where(lane == count * count + sub, column, packed)
    column = jnp.sum(image * image, axis=1, keepdims=True)
    packed = jnp.where(lane == count * count + count, column, packed)
    sums[...] = jnp.broadcast_to(jnp.sum(packed, axis=0, keepdims=True), sums.shape)


def finish_kernel(size, sums, image, basis, vector_out, hessen_out):
    count, leaves = basis.shape[0], image.shape[0]
    lane = lax.broadcasted_iota(jnp.int32, (count, 128), 1)
    sub = lax.broadcasted_iota(jnp.int32, (count, 128), 0)
    totals = jnp.broadcast_to(jnp.sum(sums[...], axis=0, keepdims=True) / size, (count, 128))
    zero = jnp.zeros((count, 128), F32)
    here = lane == count * count + sub
    coef = jnp.sum(jnp.where(here, totals, zero), axis=1, keepdims=True)
    inner = jnp.sum(jnp.where(lane % count == sub, coef, zero), axis=0, keepdims=True)
    outer = jnp.sum(jnp.where(lane // count == sub, coef, zero), axis=0, keepdims=True)
    gram = jnp.where(lane[:1] < count * count, totals[:1] * inner * outer, zero[:1])
    length = jnp.where(lane[:1] == count * count + count, totals[:1], zero[:1])
    squared = jnp.sum(gram + length, axis=1, keepdims=True)
    squared = squared - 2.0 * jnp.sum(coef * coef, axis=0, keepdims=True)
    beta = jnp.sqrt(squared + 1e-06)
    for i in range(leaves):
        taken = jnp.sum(coef * basis[:, i * PANEL : (i + 1) * PANEL], axis=0, keepdims=True)
        row = (image[i : i + 1, :] - taken) / beta
        vector_out[2 * i : 2 * i + 1, :] = row[:, : PANEL // 2]
        vector_out[2 * i + 1 : 2 * i + 2, :] = row[:, PANEL // 2 :]
    values = jnp.sum(jnp.where(lane == sub, coef, zero), axis=0, keepdims=True)
    hessen_out[...] = jnp.where(lane[:1] == count, beta, values)


def call(kernel, specs, outs, scratch=()):
    shapes = [jax.ShapeDtypeStruct(shape, dtype) for shape, dtype in outs]
    return pl.pallas_call(
        kernel,
        out_shape=shapes,
        in_specs=specs,
        out_specs=[VMEM] * len(shapes),
        scratch_shapes=list(scratch),
        compiler_params=pltpu.CompilerParams(vmem_limit_bytes=24 << 20),
    )


def like(array):
    return pltpu.VMEM(array.shape, array.dtype)


def body(
    basis, roots, near_blocks, near_ids, leaf_basis, far_coupling, far_ids, transfer, top_coupling, top_ids
):
    leaves, nears = near_blocks.shape[:2]
    fars, parents, tops = far_coupling.shape[1], *top_coupling.shape[:2]
    devices = lax.axis_size("grp") * lax.axis_size("leaf")
    mates = [(i, i ^ 1) for i in range(devices)]
    others = [(i, (((i + 1) ^ 1) - 1) % devices) for i in range(devices)]

    product, stack, basis, leaf_basis, transfer = call(
        start_kernel,
        [HBM] * 3,
        [((leaves, PANEL), F32), ((leaves, WIDTH), BF16)] + [(a.shape, a.dtype) for a in (basis, leaf_basis, transfer)],
        [pltpu.SemaphoreType.DMA((3,))],
    )(basis, leaf_basis, transfer)
    far = lax.ppermute(stack, AXES, others)
    mate = lax.ppermute(stack, AXES, mates)
    roots = roots.reshape(1, -1)
    scales, near, coupling, top, *picks = call(
        prepare_kernel,
        [VMEM] + [HBM] * 7,
        [
            ((roots.shape[1] * leaves, PANEL), F32),
            (near_blocks.shape, BF16),
            ((fars * RANK, leaves * RANK), BF16),
            ((tops * PRANK, parents * PRANK), BF16),
            ((nears * leaves, SOURCES), BF16),
            ((fars * leaves, SOURCES), BF16),
            ((tops * leaves, SOURCES), BF16),
        ],
        [like(a) for a in (roots, near_blocks, far_coupling, top_coupling, near_ids, far_ids, top_ids)]
        + [pltpu.SemaphoreType.DMA((6 + leaves,))],
    )(product, roots, near_blocks, near_ids, far_coupling, far_ids, top_coupling, top_ids)
    matrices = (*picks, near, leaf_basis, coupling, transfer, top)
    partial = product
    steps = roots.shape[1] - 1
    for step in range(steps):
        product, partial, stack = call(
            functools.partial(step_kernel, step, step == steps - 1),
            [VMEM] * 14,
            [((leaves, PANEL), F32), ((leaves, PANEL), F32), ((leaves, WIDTH), BF16)],
        )(scales, product, partial, stack, mate, far, *matrices)
        far = lax.ppermute(stack, AXES, others)
        mate = lax.ppermute(stack, AXES, mates)
    image, sums = call(
        last_kernel, [VMEM] * 13, [((leaves, PANEL), F32), ((devices, 128), F32)]
    )(partial, stack, mate, far, *matrices, basis)
    sums = lax.all_to_all(sums.reshape(devices, 1, 128), AXES, 0, 0, tiled=True)
    size = float(leaves * PANEL * devices)
    vector, hessen = call(
        functools.partial(finish_kernel, size), [VMEM] * 3, [((leaves * 2, 128), F32), ((1, 128), F32)]
    )(sums.reshape(devices, 128), image, basis)
    return vector.reshape(leaves * PANEL), hessen[0, : basis.shape[0] + 1]


def solution(mesh):
    split = P(AXES)
    in_specs = (P(None, AXES), P()) + (split,) * 8
    return jax.shard_map(body, mesh=mesh, in_specs=in_specs, out_specs=(split, P()), check_vma=False)
```

```python
import functools

import jax
import jax.numpy as jnp
from jax import lax
from jax.experimental import pallas as pl
from jax.experimental.pallas import tpu as pltpu
from jax.sharding import PartitionSpec as P

AXES = ("grp", "leaf")
F32 = jnp.float32
BF16 = jnp.bfloat16
NT = (((1,), (1,)), ((), ()))
VMEM = pl.BlockSpec(memory_space=pltpu.VMEM)
HBM = pl.BlockSpec(memory_space=pltpu.HBM)
PANEL, RANK, PRANK, WIDTH = 256, 64, 128, 512
T_AT, C_AT = PANEL, PANEL + PRANK
SOURCES = 32


def dot(a, b):
    return jnp.dot(a, b, preferred_element_type=F32)


def dot_nt(a, b):
    return lax.dot_general(a, b, NT, preferred_element_type=F32)


def diagonal(value, block):
    lane = lax.broadcasted_iota(jnp.int32, value.shape, 1)
    row = lax.broadcasted_iota(jnp.int32, value.shape, 0)
    return jnp.where(lane // block == row, value, jnp.zeros_like(value))


def flat(value):
    return jnp.broadcast_to(jnp.sum(value, axis=0, keepdims=True), value.shape)


def write_stack(field, leaf_basis, transfer, stack):
    rounded = field.astype(BF16)
    stack[:, :PANEL] = rounded
    kept = diagonal(dot_nt(rounded, leaf_basis), RANK)
    folded = sum(kept[:, at : at + 2 * RANK] for at in range(0, kept.shape[1], 2 * RANK))
    coeffs = folded[:, :RANK] + folded[:, RANK:]
    stack[:, C_AT:] = jnp.concatenate([coeffs, jnp.zeros_like(coeffs)], axis=1).astype(BF16)
    spread = diagonal(flat(kept.astype(BF16).astype(F32)), 2 * RANK)
    stack[:, T_AT:C_AT] = dot(spread.astype(BF16), transfer).astype(BF16)


def tiles(value, rows):
    return jnp.concatenate([value[at : at + rows] for at in range(0, value.shape[0], rows)], axis=1)


def apply_rows(field, own, mate, far, pick_near, pick_far, pick_top, near, leaf_basis, coupling, transfer, top):
    leaves = field.shape[0]
    rest = jnp.zeros((SOURCES - 3 * leaves, WIDTH), F32)
    window = jnp.concatenate(
        [own[...].astype(F32), mate[...].astype(F32), far[...].astype(F32), rest], axis=0
    ).astype(BF16)
    parents = tiles(dot(pick_top[...], window[:, T_AT:C_AT]), leaves).astype(BF16)
    coeffs = tiles(dot(pick_far[...], window[:, C_AT : C_AT + RANK]), leaves).astype(BF16)
    panels = dot(pick_near[...], window[:, :PANEL]).astype(BF16)
    tops = diagonal(dot(parents, top[...]), PRANK)
    tops = sum(tops[:, at : at + PRANK] for at in range(0, tops.shape[1], PRANK)).astype(BF16)
    local = diagonal(dot(coeffs, coupling[...]), RANK) + diagonal(dot_nt(tops, transfer), 2 * RANK)
    total = dot(diagonal(flat(local), RANK).astype(BF16), leaf_basis)
    row = lax.broadcasted_iota(jnp.int32, total.shape, 0)
    for i in range(leaves):
        image = jnp.zeros(total.shape, F32)
        for k in range(near.shape[1]):
            image += dot(panels[k * leaves : (k + 1) * leaves], near[i, k])
        total += jnp.where(row == i, image, jnp.zeros_like(image))
    return 0.5 * field + total


def stacked(ref):
    return ref[...].reshape(ref.shape[0] * ref.shape[1], ref.shape[2])


def start_kernel(basis, leaf_basis, transfer, product, stack, basis_in, leaf_basis_in, transfer_in, sems):
    copies = [
        pltpu.make_async_copy(source, target, sems.at[n])
        for n, (source, target) in enumerate(
            ((basis, basis_in), (leaf_basis, leaf_basis_in), (transfer, transfer_in))
        )
    ]
    for copy in copies:
        copy.start()
    for copy in copies:
        copy.wait()
    count = basis.shape[0]
    for i in range(product.shape[0]):
        product[i : i + 1, :] = basis_in[count - 1 : count, i * PANEL : (i + 1) * PANEL]
    write_stack(product[...], stacked(leaf_basis_in), stacked(transfer_in), stack)


def prepare_kernel(
    _, roots, near, near_ids, coupling, far_ids, top, top_ids,
    scales, near_out, coupling_out, top_out, pick_near, pick_far, pick_top,
    roots_in, near_in, coupling_in, top_in, near_ids_in, far_ids_in, top_ids_in, sems,
):
    leaves = near.shape[0]
    pairs = [
        (roots, roots_in), (near_ids, near_ids_in), (far_ids, far_ids_in), (top_ids, top_ids_in),
        (coupling, coupling_in), (top, top_in),
    ] + [(near.at[i], near_in.at[i]) for i in range(leaves)]
    copies = [
        pltpu.make_async_copy(source, target, sems.at[n]) for n, (source, target) in enumerate(pairs)
    ]
    for copy in copies:
        copy.start()
    for copy in copies[:4]:
        copy.wait()
    for k in range(roots.shape[1]):
        scales[k * leaves : (k + 1) * leaves, :] = jnp.broadcast_to(
            roots_in[:, k : k + 1], (leaves, scales.shape[1])
        )
    place = lax.axis_index(AXES)
    odd = place % 2 == 1
    left, right = jnp.where(odd, leaves, 2 * leaves), jnp.where(odd, 2 * leaves, leaves)
    for ids_in, pick, rows in (
        (near_ids_in, pick_near, leaves), (far_ids_in, pick_far, leaves), (top_ids_in, pick_top, leaves // 2),
    ):
        away = ids_in[...] - place * rows
        where = jnp.where(away < 0, away + rows + left, jnp.where(away < rows, away, away - rows + right))
        lane = lax.broadcasted_iota(jnp.int32, (rows, SOURCES), 1)
        for k in range(ids_in.shape[1]):
            hot = jnp.where(lane == where[:, k : k + 1], 1.0, 0.0)
            if rows < leaves:
                hot = jnp.concatenate([hot, jnp.zeros((leaves - rows, SOURCES), F32)], axis=0)
            pick[k * leaves : (k + 1) * leaves, :] = hot.astype(BF16)
    copies[4].wait()
    for i in range(leaves):
        for k in range(coupling.shape[1]):
            rows, lanes = slice(k * RANK, (k + 1) * RANK), slice(i * RANK, (i + 1) * RANK)
            coupling_out[rows, lanes] = coupling_in[i, k].T
    copies[5].wait()
    for p in range(top.shape[0]):
        for k in range(top.shape[1]):
            rows, lanes = slice(k * PRANK, (k + 1) * PRANK), slice(p * PRANK, (p + 1) * PRANK)
            top_out[rows, lanes] = top_in[p, k].T
    for i in range(leaves):
        copies[6 + i].wait()
        for k in range(near.shape[1]):
            near_out[i, k] = near_in[i, k].T


def step_kernel(
    step, last, scales, product, partial, own, mate, far, pick_near, pick_far, pick_top,
    near, leaf_basis, coupling, transfer, top, product_out, partial_out, stack,
):
    leaves = product.shape[0]
    basis_rows, transfer_rows = stacked(leaf_basis), stacked(transfer)
    field = product[...]
    image = apply_rows(
        field, own, mate, far, pick_near, pick_far, pick_top, near, basis_rows, coupling, transfer_rows, top
    )
    root = scales[step * leaves : (step + 1) * leaves, :]
    after = field - image / root
    total = field / root
    if step:
        total += partial[...]
    if last:
        total += after / scales[(step + 1) * leaves : (step + 2) * leaves, :]
    product_out[...] = after
    partial_out[...] = total
    write_stack(total if last else after, basis_rows, transfer_rows, stack)


def last_kernel(
    field, own, mate, far, pick_near, pick_far, pick_top,
    near, leaf_basis, coupling, transfer, top, basis, image_out, sums,
):
    image = apply_rows(
        field[...], own, mate, far, pick_near, pick_far, pick_top,
        near, stacked(leaf_basis), coupling, stacked(transfer), top,
    )
    image_out[...] = image
    count, leaves = basis.shape[0], image.shape[0]
    lane = lax.broadcasted_iota(jnp.int32, (count, 128), 1)
    sub = lax.broadcasted_iota(jnp.int32, (count, 128), 0)
    vectors = basis[...]
    packed = jnp.zeros((count, 128), F32)
    for n in range(count):
        column = jnp.sum(vectors * vectors[n : n + 1], axis=1, keepdims=True)
        packed = jnp.where(lane == n * count + sub, column, packed)
    dots = jnp.zeros((count, PANEL), F32)
    for i in range(leaves):
        dots += basis[:, i * PANEL : (i + 1) * PANEL] * image[i : i + 1]
    column = jnp.sum(dots, axis=1, keepdims=True)
    packed = jnp.where(lane == count * count + sub, column, packed)
    column = jnp.sum(image * image, axis=1, keepdims=True)
    packed = jnp.where(lane == count * count + count, column, packed)
    sums[...] = jnp.broadcast_to(jnp.sum(packed, axis=0, keepdims=True), sums.shape)


def finish_kernel(size, sums, image, basis, vector_out, hessen_out):
    count, leaves = basis.shape[0], image.shape[0]
    lane = lax.broadcasted_iota(jnp.int32, (count, 128), 1)
    sub = lax.broadcasted_iota(jnp.int32, (count, 128), 0)
    totals = jnp.broadcast_to(jnp.sum(sums[...], axis=0, keepdims=True) / size, (count, 128))
    zero = jnp.zeros((count, 128), F32)
    here = lane == count * count + sub
    coef = jnp.sum(jnp.where(here, totals, zero), axis=1, keepdims=True)
    inner = jnp.sum(jnp.where(lane % count == sub, coef, zero), axis=0, keepdims=True)
    outer = jnp.sum(jnp.where(lane // count == sub, coef, zero), axis=0, keepdims=True)
    gram = jnp.where(lane[:1] < count * count, totals[:1] * inner * outer, zero[:1])
    length = jnp.where(lane[:1] == count * count + count, totals[:1], zero[:1])
    squared = jnp.sum(gram + length, axis=1, keepdims=True)
    squared = squared - 2.0 * jnp.sum(coef * coef, axis=0, keepdims=True)
    beta = jnp.sqrt(squared + 1e-06)
    for i in range(leaves):
        taken = jnp.sum(coef * basis[:, i * PANEL : (i + 1) * PANEL], axis=0, keepdims=True)
        row = (image[i : i + 1, :] - taken) / beta
        vector_out[2 * i : 2 * i + 1, :] = row[:, : PANEL // 2]
        vector_out[2 * i + 1 : 2 * i + 2, :] = row[:, PANEL // 2 :]
    values = jnp.sum(jnp.where(lane == sub, coef, zero), axis=0, keepdims=True)
    hessen_out[...] = jnp.where(lane[:1] == count, beta, values)


def call(kernel, specs, outs, scratch=()):
    shapes = [jax.ShapeDtypeStruct(shape, dtype) for shape, dtype in outs]
    return pl.pallas_call(
        kernel,
        out_shape=shapes,
        in_specs=specs,
        out_specs=[VMEM] * len(shapes),
        scratch_shapes=list(scratch),
        compiler_params=pltpu.CompilerParams(vmem_limit_bytes=24 << 20),
    )


def pinned(*arrays):
    return [pltpu.with_memory_space_constraint(a, pltpu.HBM) for a in arrays]


def like(array):
    return pltpu.VMEM(array.shape, array.dtype)


def body(
    basis, roots, near_blocks, near_ids, leaf_basis, far_coupling, far_ids, transfer, top_coupling, top_ids
):
    leaves, nears = near_blocks.shape[:2]
    fars, parents, tops = far_coupling.shape[1], *top_coupling.shape[:2]
    devices = lax.axis_size("grp") * lax.axis_size("leaf")
    mates = [(i, i ^ 1) for i in range(devices)]
    others = [(i, (((i + 1) ^ 1) - 1) % devices) for i in range(devices)]

    product, stack, basis, leaf_basis, transfer = call(
        start_kernel,
        [HBM] * 3,
        [((leaves, PANEL), F32), ((leaves, WIDTH), BF16)] + [(a.shape, a.dtype) for a in (basis, leaf_basis, transfer)],
        [pltpu.SemaphoreType.DMA((3,))],
    )(*pinned(basis, leaf_basis, transfer))
    far = lax.ppermute(stack, AXES, others)
    mate = lax.ppermute(stack, AXES, mates)
    roots = roots.reshape(1, -1)
    scales, near, coupling, top, *picks = call(
        prepare_kernel,
        [VMEM] + [HBM] * 7,
        [
            ((roots.shape[1] * leaves, PANEL), F32),
            (near_blocks.shape, BF16),
            ((fars * RANK, leaves * RANK), BF16),
            ((tops * PRANK, parents * PRANK), BF16),
            ((nears * leaves, SOURCES), BF16),
            ((fars * leaves, SOURCES), BF16),
            ((tops * leaves, SOURCES), BF16),
        ],
        [like(a) for a in (roots, near_blocks, far_coupling, top_coupling, near_ids, far_ids, top_ids)]
        + [pltpu.SemaphoreType.DMA((6 + leaves,))],
    )(product, *pinned(roots, near_blocks, near_ids, far_coupling, far_ids, top_coupling, top_ids))
    matrices = (*picks, near, leaf_basis, coupling, transfer, top)
    partial = product
    steps = roots.shape[1] - 1
    for step in range(steps):
        product, partial, stack = call(
            functools.partial(step_kernel, step, step == steps - 1),
            [VMEM] * 14,
            [((leaves, PANEL), F32), ((leaves, PANEL), F32), ((leaves, WIDTH), BF16)],
        )(scales, product, partial, stack, mate, far, *matrices)
        far = lax.ppermute(stack, AXES, others)
        mate = lax.ppermute(stack, AXES, mates)
    image, sums = call(
        last_kernel, [VMEM] * 13, [((leaves, PANEL), F32), ((devices, 128), F32)]
    )(partial, stack, mate, far, *matrices, basis)
    sums = lax.all_to_all(sums.reshape(devices, 1, 128), AXES, 0, 0, tiled=True)
    size = float(leaves * PANEL * devices)
    vector, hessen = call(
        functools.partial(finish_kernel, size), [VMEM] * 3, [((leaves * 2, 128), F32), ((1, 128), F32)]
    )(sums.reshape(devices, 128), image, basis)
    return vector.reshape(leaves * PANEL), hessen[0, : basis.shape[0] + 1]


def solution(mesh):
    split = P(AXES)
    in_specs = (P(None, AXES), P()) + (split,) * 8
    return jax.shard_map(body, mesh=mesh, in_specs=in_specs, out_specs=(split, P()), check_vma=False)
```

```python
import functools

import jax
import jax.numpy as jnp
from jax import lax
from jax.experimental import pallas as pl
from jax.experimental.pallas import tpu as pltpu
from jax.sharding import PartitionSpec as P

AXES = ("grp", "leaf")
F32 = jnp.float32
BF16 = jnp.bfloat16
NT = (((1,), (1,)), ((), ()))
VMEM = pl.BlockSpec(memory_space=pltpu.VMEM)
HBM = pl.BlockSpec(memory_space=pltpu.HBM)
PANEL, RANK, PRANK, WIDTH = 256, 64, 128, 512
T_AT, C_AT = PANEL, PANEL + PRANK
SOURCES = 32


def dot(a, b):
    return jnp.dot(a, b, preferred_element_type=F32)


def dot_nt(a, b):
    return lax.dot_general(a, b, NT, preferred_element_type=F32)


def diagonal(value, block):
    lane = lax.broadcasted_iota(jnp.int32, value.shape, 1)
    row = lax.broadcasted_iota(jnp.int32, value.shape, 0)
    return jnp.where(lane // block == row, value, jnp.zeros_like(value))


def flat(value):
    return jnp.broadcast_to(jnp.sum(value, axis=0, keepdims=True), value.shape)


def write_stack(field, leaf_basis, transfer, stack):
    rounded = field.astype(BF16)
    stack[:, :PANEL] = rounded
    kept = diagonal(dot_nt(rounded, leaf_basis), RANK)
    folded = sum(kept[:, at : at + 2 * RANK] for at in range(0, kept.shape[1], 2 * RANK))
    coeffs = folded[:, :RANK] + folded[:, RANK:]
    stack[:, C_AT:] = jnp.concatenate([coeffs, jnp.zeros_like(coeffs)], axis=1).astype(BF16)
    spread = diagonal(flat(kept.astype(BF16).astype(F32)), 2 * RANK)
    stack[:, T_AT:C_AT] = dot(spread.astype(BF16), transfer).astype(BF16)


def tiles(value, rows):
    return jnp.concatenate([value[at : at + rows] for at in range(0, value.shape[0], rows)], axis=1)


def apply_rows(field, own, mate, far, pick_near, pick_far, pick_top, near, leaf_basis, coupling, transfer, top):
    leaves = field.shape[0]
    rest = jnp.zeros((SOURCES - 3 * leaves, WIDTH), F32)
    window = jnp.concatenate(
        [own[...].astype(F32), mate[...].astype(F32), far[...].astype(F32), rest], axis=0
    ).astype(BF16)
    parents = tiles(dot(pick_top[...], window[:, T_AT:C_AT]), leaves).astype(BF16)
    coeffs = tiles(dot(pick_far[...], window[:, C_AT : C_AT + RANK]), leaves).astype(BF16)
    panels = dot(pick_near[...], window[:, :PANEL]).astype(BF16)
    tops = diagonal(dot(parents, top[...]), PRANK)
    tops = sum(tops[:, at : at + PRANK] for at in range(0, tops.shape[1], PRANK)).astype(BF16)
    local = diagonal(dot(coeffs, coupling[...]), RANK) + diagonal(dot_nt(tops, transfer), 2 * RANK)
    total = dot(diagonal(flat(local), RANK).astype(BF16), leaf_basis)
    row = lax.broadcasted_iota(jnp.int32, total.shape, 0)
    for i in range(leaves):
        image = jnp.zeros(total.shape, F32)
        for k in range(near.shape[1]):
            image += dot(panels[k * leaves : (k + 1) * leaves], near[i, k])
        total += jnp.where(row == i, image, jnp.zeros_like(image))
    return 0.5 * field + total


def stacked(ref):
    return ref[...].reshape(ref.shape[0] * ref.shape[1], ref.shape[2])


def start_kernel(basis, leaf_basis, transfer, product, stack, basis_in, leaf_basis_in, transfer_in, sems):
    copies = [
        pltpu.make_async_copy(source, target, sems.at[n])
        for n, (source, target) in enumerate(
            ((basis, basis_in), (leaf_basis, leaf_basis_in), (transfer, transfer_in))
        )
    ]
    for copy in copies:
        copy.start()
    for copy in copies:
        copy.wait()
    count = basis.shape[0]
    for i in range(product.shape[0]):
        product[i : i + 1, :] = basis_in[count - 1 : count, i * PANEL : (i + 1) * PANEL]
    write_stack(product[...], stacked(leaf_basis_in), stacked(transfer_in), stack)


def prepare_kernel(
    _, roots, near, near_ids, coupling, far_ids, top, top_ids,
    scales, near_out, coupling_out, top_out, pick_near, pick_far, pick_top,
    roots_in, near_in, coupling_in, top_in, near_ids_in, far_ids_in, top_ids_in, sems,
):
    leaves = near.shape[0]
    pairs = [
        (roots, roots_in), (near_ids, near_ids_in), (far_ids, far_ids_in), (top_ids, top_ids_in),
        (coupling, coupling_in), (top, top_in),
    ] + [(near.at[i], near_in.at[i]) for i in range(leaves)]
    copies = [
        pltpu.make_async_copy(source, target, sems.at[n]) for n, (source, target) in enumerate(pairs)
    ]
    for copy in copies:
        copy.start()
    for copy in copies[:4]:
        copy.wait()
    for k in range(roots.shape[1]):
        scales[k * leaves : (k + 1) * leaves, :] = jnp.broadcast_to(
            roots_in[:, k : k + 1], (leaves, scales.shape[1])
        )
    place = lax.axis_index(AXES)
    odd = place % 2 == 1
    left, right = jnp.where(odd, leaves, 2 * leaves), jnp.where(odd, 2 * leaves, leaves)
    for ids_in, pick, rows in (
        (near_ids_in, pick_near, leaves), (far_ids_in, pick_far, leaves), (top_ids_in, pick_top, leaves // 2),
    ):
        away = ids_in[...] - place * rows
        where = jnp.where(away < 0, away + rows + left, jnp.where(away < rows, away, away - rows + right))
        lane = lax.broadcasted_iota(jnp.int32, (rows, SOURCES), 1)
        for k in range(ids_in.shape[1]):
            hot = jnp.where(lane == where[:, k : k + 1], 1.0, 0.0)
            if rows < leaves:
                hot = jnp.concatenate([hot, jnp.zeros((leaves - rows, SOURCES), F32)], axis=0)
            pick[k * leaves : (k + 1) * leaves, :] = hot.astype(BF16)
    copies[4].wait()
    for i in range(leaves):
        for k in range(coupling.shape[1]):
            rows, lanes = slice(k * RANK, (k + 1) * RANK), slice(i * RANK, (i + 1) * RANK)
            coupling_out[rows, lanes] = coupling_in[i, k].T
    copies[5].wait()
    for p in range(top.shape[0]):
        for k in range(top.shape[1]):
            rows, lanes = slice(k * PRANK, (k + 1) * PRANK), slice(p * PRANK, (p + 1) * PRANK)
            top_out[rows, lanes] = top_in[p, k].T
    for i in range(leaves):
        copies[6 + i].wait()
        for k in range(near.shape[1]):
            near_out[i, k] = near_in[i, k].T


def at_an_end():
    place = lax.axis_index(AXES)
    return jnp.logical_or(place == 0, place == lax.axis_size(AXES) - 1)


def advance(step, last, image, field, scales, partial, leaf_basis, transfer, product_out, partial_out, stack):
    leaves = field.shape[0]
    root = scales[step * leaves : (step + 1) * leaves, :]
    after = field - image / root
    total = field / root
    if step:
        total += partial[...]
    if last:
        total += after / scales[(step + 1) * leaves : (step + 2) * leaves, :]
    product_out[...] = after
    partial_out[...] = total
    write_stack(total if last else after, leaf_basis, transfer, stack)


def step_kernel(
    step, last, early, scales, product, partial, own, mate, far, picks, matrices, outs, ready=()
):
    near, leaf_basis, coupling, transfer, top = matrices

    @pl.when(at_an_end() if early else jnp.logical_not(at_an_end()))
    def _():
        basis_rows, transfer_rows = stacked(leaf_basis), stacked(transfer)
        field = product[...]
        image = apply_rows(
            field, own, mate, far, *picks, near, basis_rows, coupling, transfer_rows, top
        )
        advance(step, last, image, field, scales, partial, basis_rows, transfer_rows, *outs)

    if not early:

        @pl.when(at_an_end())
        def _():
            for source, target in zip(ready, outs):
                target[...] = source[...]


def step_early(step, last, scales, product, partial, own, mate, *rest):
    step_kernel(step, last, True, scales, product, partial, own, mate, own, rest[:3], rest[3:8], rest[8:])


def step_late(step, last, scales, product, partial, own, mate, far, *rest):
    picks, matrices, ready, outs = rest[:3], rest[3:8], rest[8:11], rest[11:]
    step_kernel(step, last, False, scales, product, partial, own, mate, far, picks, matrices, outs, ready)


def last_image(early, field, own, mate, far, picks, matrices, image_out):
    near, leaf_basis, coupling, transfer, top = matrices

    @pl.when(at_an_end() if early else jnp.logical_not(at_an_end()))
    def _():
        image_out[...] = apply_rows(
            field[...], own, mate, far, *picks, near, stacked(leaf_basis), coupling, stacked(transfer), top
        )


def last_early(field, own, mate, *rest):
    last_image(True, field, own, mate, own, rest[:3], rest[3:8], rest[8])


def last_late(field, own, mate, far, *rest):
    picks, matrices, (basis, ready, image_out, sums) = rest[:3], rest[3:8], rest[8:]
    last_image(False, field, own, mate, far, picks, matrices, image_out)

    @pl.when(at_an_end())
    def _():
        image_out[...] = ready[...]

    image = image_out[...]
    count, leaves = basis.shape[0], image.shape[0]
    lane = lax.broadcasted_iota(jnp.int32, (count, 128), 1)
    sub = lax.broadcasted_iota(jnp.int32, (count, 128), 0)
    vectors = basis[...]
    packed = jnp.zeros((count, 128), F32)
    for n in range(count):
        column = jnp.sum(vectors * vectors[n : n + 1], axis=1, keepdims=True)
        packed = jnp.where(lane == n * count + sub, column, packed)
    dots = jnp.zeros((count, PANEL), F32)
    for i in range(leaves):
        dots += basis[:, i * PANEL : (i + 1) * PANEL] * image[i : i + 1]
    column = jnp.sum(dots, axis=1, keepdims=True)
    packed = jnp.where(lane == count * count + sub, column, packed)
    column = jnp.sum(image * image, axis=1, keepdims=True)
    packed = jnp.where(lane == count * count + count, column, packed)
    sums[...] = jnp.broadcast_to(jnp.sum(packed, axis=0, keepdims=True), sums.shape)


def finish_kernel(size, sums, image, basis, vector_out, hessen_out):
    count, leaves = basis.shape[0], image.shape[0]
    lane = lax.broadcasted_iota(jnp.int32, (count, 128), 1)
    sub = lax.broadcasted_iota(jnp.int32, (count, 128), 0)
    totals = jnp.broadcast_to(jnp.sum(sums[...], axis=0, keepdims=True) / size, (count, 128))
    zero = jnp.zeros((count, 128), F32)
    here = lane == count * count + sub
    coef = jnp.sum(jnp.where(here, totals, zero), axis=1, keepdims=True)
    inner = jnp.sum(jnp.where(lane % count == sub, coef, zero), axis=0, keepdims=True)
    outer = jnp.sum(jnp.where(lane // count == sub, coef, zero), axis=0, keepdims=True)
    gram = jnp.where(lane[:1] < count * count, totals[:1] * inner * outer, zero[:1])
    length = jnp.where(lane[:1] == count * count + count, totals[:1], zero[:1])
    squared = jnp.sum(gram + length, axis=1, keepdims=True)
    squared = squared - 2.0 * jnp.sum(coef * coef, axis=0, keepdims=True)
    beta = jnp.sqrt(squared + 1e-06)
    for i in range(leaves):
        taken = jnp.sum(coef * basis[:, i * PANEL : (i + 1) * PANEL], axis=0, keepdims=True)
        row = (image[i : i + 1, :] - taken) / beta
        vector_out[2 * i : 2 * i + 1, :] = row[:, : PANEL // 2]
        vector_out[2 * i + 1 : 2 * i + 2, :] = row[:, PANEL // 2 :]
    values = jnp.sum(jnp.where(lane == sub, coef, zero), axis=0, keepdims=True)
    hessen_out[...] = jnp.where(lane[:1] == count, beta, values)


def call(kernel, specs, outs, scratch=()):
    shapes = [jax.ShapeDtypeStruct(shape, dtype) for shape, dtype in outs]
    return pl.pallas_call(
        kernel,
        out_shape=shapes,
        in_specs=specs,
        out_specs=[VMEM] * len(shapes),
        scratch_shapes=list(scratch),
        compiler_params=pltpu.CompilerParams(vmem_limit_bytes=24 << 20),
    )


def pinned(*arrays):
    return [pltpu.with_memory_space_constraint(a, pltpu.HBM) for a in arrays]


def like(array):
    return pltpu.VMEM(array.shape, array.dtype)


def body(
    basis, roots, near_blocks, near_ids, leaf_basis, far_coupling, far_ids, transfer, top_coupling, top_ids
):
    leaves, nears = near_blocks.shape[:2]
    fars, parents, tops = far_coupling.shape[1], *top_coupling.shape[:2]
    devices = lax.axis_size("grp") * lax.axis_size("leaf")
    mates = [(i, i ^ 1) for i in range(devices)]
    others = [(i, (((i + 1) ^ 1) - 1) % devices) for i in range(devices)]

    product, stack, basis, leaf_basis, transfer = call(
        start_kernel,
        [HBM] * 3,
        [((leaves, PANEL), F32), ((leaves, WIDTH), BF16)] + [(a.shape, a.dtype) for a in (basis, leaf_basis, transfer)],
        [pltpu.SemaphoreType.DMA((3,))],
    )(*pinned(basis, leaf_basis, transfer))
    far = lax.ppermute(stack, AXES, others)
    mate = lax.ppermute(stack, AXES, mates)
    roots = roots.reshape(1, -1)
    scales, near, coupling, top, *picks = call(
        prepare_kernel,
        [VMEM] + [HBM] * 7,
        [
            ((roots.shape[1] * leaves, PANEL), F32),
            (near_blocks.shape, BF16),
            ((fars * RANK, leaves * RANK), BF16),
            ((tops * PRANK, parents * PRANK), BF16),
            ((nears * leaves, SOURCES), BF16),
            ((fars * leaves, SOURCES), BF16),
            ((tops * leaves, SOURCES), BF16),
        ],
        [like(a) for a in (roots, near_blocks, far_coupling, top_coupling, near_ids, far_ids, top_ids)]
        + [pltpu.SemaphoreType.DMA((6 + leaves,))],
    )(product, *pinned(roots, near_blocks, near_ids, far_coupling, far_ids, top_coupling, top_ids))
    matrices = (*picks, near, leaf_basis, coupling, transfer, top)
    partial = product
    steps = roots.shape[1] - 1
    outs = [((leaves, PANEL), F32), ((leaves, PANEL), F32), ((leaves, WIDTH), BF16)]
    for step in range(steps):
        last = step == steps - 1
        state = (scales, product, partial, stack, mate)
        ready = call(functools.partial(step_early, step, last), [VMEM] * 13, outs)(*state, *matrices)
        product, partial, stack = call(functools.partial(step_late, step, last), [VMEM] * 17, outs)(
            *state, far, *matrices, *ready
        )
        far = lax.ppermute(stack, AXES, others)
        mate = lax.ppermute(stack, AXES, mates)
    state = (partial, stack, mate)
    ready = call(last_early, [VMEM] * 11, outs[:1])(*state, *matrices)
    image, sums = call(last_late, [VMEM] * 14, [outs[0], ((devices, 128), F32)])(
        *state, far, *matrices, basis, *ready
    )
    sums = lax.all_to_all(sums.reshape(devices, 1, 128), AXES, 0, 0, tiled=True)
    size = float(leaves * PANEL * devices)
    vector, hessen = call(
        functools.partial(finish_kernel, size), [VMEM] * 3, [((leaves * 2, 128), F32), ((1, 128), F32)]
    )(sums.reshape(devices, 128), image, basis)
    return vector.reshape(leaves * PANEL), hessen[0, : basis.shape[0] + 1]


def solution(mesh):
    split = P(AXES)
    in_specs = (P(None, AXES), P()) + (split,) * 8
    return jax.shard_map(body, mesh=mesh, in_specs=in_specs, out_specs=(split, P()), check_vma=False)
```

```python
import functools

import jax
import jax.numpy as jnp
from jax import lax
from jax.experimental import pallas as pl
from jax.experimental.pallas import tpu as pltpu
from jax.sharding import PartitionSpec as P

AXES = ("grp", "leaf")
F32 = jnp.float32
BF16 = jnp.bfloat16
NT = (((1,), (1,)), ((), ()))
VMEM = pl.BlockSpec(memory_space=pltpu.VMEM)
HBM = pl.BlockSpec(memory_space=pltpu.HBM)
PANEL, RANK, PRANK, WIDTH = 256, 64, 128, 512
T_AT, C_AT = PANEL, PANEL + PRANK
SOURCES = 32
SLOTS = 18


def dot(a, b):
    return jnp.dot(a, b, preferred_element_type=F32)


def dot_nt(a, b):
    return lax.dot_general(a, b, NT, preferred_element_type=F32)


def diagonal(value, block):
    lane = lax.broadcasted_iota(jnp.int32, value.shape, 1)
    row = lax.broadcasted_iota(jnp.int32, value.shape, 0)
    return jnp.where(lane // block == row, value, jnp.zeros_like(value))


def flat(value):
    return jnp.broadcast_to(jnp.sum(value, axis=0, keepdims=True), value.shape)


def write_stack(field, leaf_basis, transfer, stack):
    rounded = field.astype(BF16)
    stack[:, :PANEL] = rounded
    kept = diagonal(dot_nt(rounded, leaf_basis), RANK)
    folded = sum(kept[:, at : at + 2 * RANK] for at in range(0, kept.shape[1], 2 * RANK))
    coeffs = folded[:, :RANK] + folded[:, RANK:]
    stack[:, C_AT:] = jnp.concatenate([coeffs, jnp.zeros_like(coeffs)], axis=1).astype(BF16)
    spread = diagonal(flat(kept.astype(BF16).astype(F32)), 2 * RANK)
    stack[:, T_AT:C_AT] = dot(spread.astype(BF16), transfer).astype(BF16)


def tiles(value, rows):
    return jnp.concatenate([value[at : at + rows] for at in range(0, value.shape[0], rows)], axis=1)


def window_of(*stacks):
    rest = jnp.zeros((SOURCES - sum(part.shape[0] for part in stacks), WIDTH), F32)
    return jnp.concatenate([part.astype(F32) for part in stacks] + [rest], axis=0).astype(BF16)


def far_sums(window, pick_far, pick_top, coupling, top):
    leaves = pick_far.shape[0] // (coupling.shape[0] // RANK)
    parents = tiles(dot(pick_top[...], window[:, T_AT:C_AT]), leaves).astype(BF16)
    coeffs = tiles(dot(pick_far[...], window[:, C_AT : C_AT + RANK]), leaves).astype(BF16)
    tops = diagonal(dot(parents, top[...]), PRANK)
    tops = sum(tops[:, at : at + PRANK] for at in range(0, tops.shape[1], PRANK))
    return tops, diagonal(dot(coeffs, coupling[...]), RANK)


def far_rows(tops, local, leaf_basis, transfer):
    local = local + diagonal(dot_nt(tops.astype(BF16), transfer), 2 * RANK)
    return dot(diagonal(flat(local), RANK).astype(BF16), leaf_basis)


def near_rows(window, pick_near, near):
    leaves = near.shape[0]
    panels = dot(pick_near[...], window[:, :PANEL]).astype(BF16)
    total = jnp.zeros((leaves, PANEL), F32)
    row = lax.broadcasted_iota(jnp.int32, total.shape, 0)
    for i in range(leaves):
        image = jnp.zeros(total.shape, F32)
        for k in range(near.shape[1]):
            image += dot(panels[k * leaves : (k + 1) * leaves], near[i, k])
        total += jnp.where(row == i, image, jnp.zeros_like(image))
    return total


def slot_rows(window, pick_slots, slots, leaves):
    panels = tiles(dot(pick_slots[...], window[:, :PANEL]), leaves).astype(BF16)
    return dot(panels, slots[:SLOTS].reshape(SLOTS * PANEL, PANEL))


def stacked(ref):
    return ref[...].reshape(ref.shape[0] * ref.shape[1], ref.shape[2])


def start_kernel(basis, leaf_basis, transfer, product, stack, basis_in, leaf_basis_in, transfer_in, sems):
    copies = [
        pltpu.make_async_copy(source, target, sems.at[n])
        for n, (source, target) in enumerate(
            ((basis, basis_in), (leaf_basis, leaf_basis_in), (transfer, transfer_in))
        )
    ]
    for copy in copies:
        copy.start()
    for copy in copies:
        copy.wait()
    count = basis.shape[0]
    for i in range(product.shape[0]):
        product[i : i + 1, :] = basis_in[count - 1 : count, i * PANEL : (i + 1) * PANEL]
    write_stack(product[...], stacked(leaf_basis_in), stacked(transfer_in), stack)


def identity(size):
    row = lax.broadcasted_iota(jnp.int32, (size, size), 0)
    return jnp.where(row == lax.broadcasted_iota(jnp.int32, (size, size), 1), 1.0, 0.0).astype(BF16)


def prepare_kernel(
    _, roots, near, near_ids, coupling, far_ids, top, top_ids,
    scales, crowded, near_out, slots, coupling_out, top_out, pick_slots, pick_near, pick_far, pick_top,
    roots_in, near_in, coupling_in, top_in, near_ids_in, far_ids_in, top_ids_in, near_ids_at, hot_rows, sems,
):
    leaves = near.shape[0]
    pairs = [
        (roots, roots_in), (near_ids, near_ids_in), (far_ids, far_ids_in), (top_ids, top_ids_in),
        (near_ids, near_ids_at), (coupling, coupling_in), (top, top_in),
    ] + [(near.at[i], near_in.at[i]) for i in range(leaves)]
    copies = [
        pltpu.make_async_copy(source, target, sems.at[n]) for n, (source, target) in enumerate(pairs)
    ]
    for copy in copies:
        copy.start()
    hot_rows[...] = jnp.zeros_like(hot_rows)
    slots[...] = jnp.zeros_like(slots)
    for copy in copies[:5]:
        copy.wait()
    for k in range(roots.shape[1]):
        scales[k * leaves : (k + 1) * leaves, :] = jnp.broadcast_to(
            roots_in[:, k : k + 1], (leaves, scales.shape[1])
        )
    place = lax.axis_index(AXES)
    odd = place % 2 == 1
    left, right = jnp.where(odd, leaves, 2 * leaves), jnp.where(odd, 2 * leaves, leaves)
    for ids_in, pick, rows in (
        (near_ids_in, pick_near, leaves), (far_ids_in, pick_far, leaves), (top_ids_in, pick_top, leaves // 2),
    ):
        away = ids_in[...] - place * rows
        where = jnp.where(away < 0, away + rows + left, jnp.where(away < rows, away, away - rows + right))
        lane = lax.broadcasted_iota(jnp.int32, (rows, SOURCES), 1)
        for k in range(ids_in.shape[1]):
            hot = jnp.where(lane == where[:, k : k + 1], 1.0, 0.0)
            if rows < leaves:
                hot = jnp.concatenate([hot, jnp.zeros((leaves - rows, SOURCES), F32)], axis=0)
            pick[k * leaves : (k + 1) * leaves, :] = hot.astype(BF16)
    copies[5].wait()
    for k in range(coupling.shape[1]):
        rows = jnp.concatenate([coupling_in[i, k] for i in range(leaves)], axis=0)
        coupling_out[k * RANK : (k + 1) * RANK, :] = rows.T
    copies[6].wait()
    for p in range(top.shape[0]):
        for k in range(top.shape[1]):
            rows, lanes = slice(k * PRANK, (k + 1) * PRANK), slice(p * PRANK, (p + 1) * PRANK)
            top_out[rows, lanes] = top_in[p, k].T
    unit = identity(PANEL)
    lane = lax.broadcasted_iota(jnp.int32, (1, hot_rows.shape[1]), 1)
    count = jnp.int32(0)
    for i in range(leaves):
        copies[7 + i].wait()
        for k in range(near.shape[1]):
            block = dot_nt(unit, near_in[i, k]).astype(BF16) if k % 2 else near_in[i, k].T
            near_out[i, k] = block
            if k == 0:
                continue
            away = near_ids_at[i, k] - place * leaves
            outside = jnp.where(odd, away >= leaves, away < 0)
            slot = jnp.where(jnp.logical_and(outside, count < SLOTS), count, SLOTS)
            slots[slot] = block
            source = jnp.where(odd, away + leaves, away + 3 * leaves)
            hot_rows[pl.ds(slot * leaves + i, 1), :] = jnp.where(lane == source, 1.0, 0.0)
            count += outside.astype(jnp.int32)
    pick_slots[...] = hot_rows[: SLOTS * leaves, :SOURCES].astype(BF16)
    crowded[...] = jnp.full(crowded.shape, jnp.maximum(count - SLOTS, 0), jnp.int32)


def at_an_end():
    place = lax.axis_index(AXES)
    return jnp.logical_or(place == 0, place == lax.axis_size(AXES) - 1)


def advance(step, last, image, field, scales, partial, leaf_basis, transfer, product_out, partial_out, stack):
    leaves = field.shape[0]
    root = scales[step * leaves : (step + 1) * leaves, :]
    after = field - image / root
    total = field / root
    if step:
        total += partial[...]
    if last:
        total += after / scales[(step + 1) * leaves : (step + 2) * leaves, :]
    product_out[...] = after
    partial_out[...] = total
    write_stack(total if last else after, leaf_basis, transfer, stack)


def early_sums(field, own, mate, picks, matrices, sums):
    near, _, coupling, _, top = matrices
    window = window_of(own[...], mate[...])
    tops, local = far_sums(window, *picks[1:], coupling, top)
    base = 0.5 * field + near_rows(window, picks[0], near)
    for target, value in zip(sums, (tops, local, base)):
        target[...] = value
    return tops, local, base


def whole_image(field, own, mate, far, picks, matrices):
    near, leaf_basis, coupling, transfer, top = matrices
    window = window_of(own[...], mate[...], far[...])
    tops, local = far_sums(window, *picks[1:], coupling, top)
    rows = far_rows(tops, local, stacked(leaf_basis), stacked(transfer))
    return 0.5 * field + near_rows(window, picks[0], near) + rows


def late_image(far, sums, pick_slots, slots, picks, matrices):
    _, leaf_basis, coupling, transfer, top = matrices
    leaves = far.shape[0]
    nothing = jnp.zeros((2 * leaves, WIDTH), F32)
    window = window_of(nothing, far[...])
    tops, local = far_sums(window, *picks[1:], coupling, top)
    rows = far_rows(tops + sums[0][...], local + sums[1][...], stacked(leaf_basis), stacked(transfer))
    return sums[2][...] + slot_rows(window, pick_slots, slots, leaves) + rows


def late_paths(crowded, late, whole, ready):
    many = jnp.max(crowded[...]) > 0
    end = at_an_end()
    inner = jnp.logical_not(end)
    pl.when(jnp.logical_and(inner, jnp.logical_not(many)))(late)
    pl.when(jnp.logical_and(inner, many))(whole)
    pl.when(end)(ready)


def step_early(step, last, scales, product, partial, own, mate, *rest):
    picks, matrices, sums, outs = rest[:3], rest[3:8], rest[8:11], rest[11:]
    field = product[...]
    tops, local, base = early_sums(field, own, mate, picks, matrices, sums)

    @pl.when(at_an_end())
    def _():
        leaf_basis, transfer = stacked(matrices[1]), stacked(matrices[3])
        image = base + far_rows(tops, local, leaf_basis, transfer)
        advance(step, last, image, field, scales, partial, leaf_basis, transfer, *outs)


def step_late(step, last, scales, product, partial, own, mate, far, crowded, pick_slots, slots, *rest):
    picks, matrices, sums, ready, outs = rest[:3], rest[3:8], rest[8:11], rest[11:14], rest[14:]

    def go_on(image):
        leaf_basis, transfer = stacked(matrices[1]), stacked(matrices[3])
        advance(step, last, image, product[...], scales, partial, leaf_basis, transfer, *outs)

    def late():
        go_on(late_image(far, sums, pick_slots, slots, picks, matrices))

    def whole():
        go_on(whole_image(product[...], own, mate, far, picks, matrices))

    def copy():
        for source, target in zip(ready, outs):
            target[...] = source[...]

    late_paths(crowded, late, whole, copy)


def last_early(field, own, mate, *rest):
    picks, matrices, sums, image_out = rest[:3], rest[3:8], rest[8:11], rest[11]
    tops, local, base = early_sums(field[...], own, mate, picks, matrices, sums)

    @pl.when(at_an_end())
    def _():
        image_out[...] = base + far_rows(tops, local, stacked(matrices[1]), stacked(matrices[3]))


def last_late(field, own, mate, far, crowded, pick_slots, slots, *rest):
    picks, matrices, early = rest[:3], rest[3:8], rest[8:11]
    ready, basis, image_out, sums = rest[11:]

    def late():
        image_out[...] = late_image(far, early, pick_slots, slots, picks, matrices)

    def whole():
        image_out[...] = whole_image(field[...], own, mate, far, picks, matrices)

    def copy():
        image_out[...] = ready[...]

    late_paths(crowded, late, whole, copy)
    image = image_out[...]
    count, leaves = basis.shape[0], image.shape[0]
    lane = lax.broadcasted_iota(jnp.int32, (count, 128), 1)
    sub = lax.broadcasted_iota(jnp.int32, (count, 128), 0)
    vectors = basis[...]
    packed = jnp.zeros((count, 128), F32)
    for n in range(count):
        column = jnp.sum(vectors * vectors[n : n + 1], axis=1, keepdims=True)
        packed = jnp.where(lane == n * count + sub, column, packed)
    dots = jnp.zeros((count, PANEL), F32)
    for i in range(leaves):
        dots += basis[:, i * PANEL : (i + 1) * PANEL] * image[i : i + 1]
    column = jnp.sum(dots, axis=1, keepdims=True)
    packed = jnp.where(lane == count * count + sub, column, packed)
    column = jnp.sum(image * image, axis=1, keepdims=True)
    packed = jnp.where(lane == count * count + count, column, packed)
    sums[...] = jnp.broadcast_to(jnp.sum(packed, axis=0, keepdims=True), sums.shape)


def finish_kernel(size, sums, image, basis, vector_out, hessen_out):
    count, leaves = basis.shape[0], image.shape[0]
    lane = lax.broadcasted_iota(jnp.int32, (count, 128), 1)
    sub = lax.broadcasted_iota(jnp.int32, (count, 128), 0)
    totals = jnp.broadcast_to(jnp.sum(sums[...], axis=0, keepdims=True) / size, (count, 128))
    zero = jnp.zeros((count, 128), F32)
    here = lane == count * count + sub
    coef = jnp.sum(jnp.where(here, totals, zero), axis=1, keepdims=True)
    inner = jnp.sum(jnp.where(lane % count == sub, coef, zero), axis=0, keepdims=True)
    outer = jnp.sum(jnp.where(lane // count == sub, coef, zero), axis=0, keepdims=True)
    gram = jnp.where(lane[:1] < count * count, totals[:1] * inner * outer, zero[:1])
    length = jnp.where(lane[:1] == count * count + count, totals[:1], zero[:1])
    squared = jnp.sum(gram + length, axis=1, keepdims=True)
    squared = squared - 2.0 * jnp.sum(coef * coef, axis=0, keepdims=True)
    beta = jnp.sqrt(squared + 1e-06)
    for i in range(leaves):
        taken = jnp.sum(coef * basis[:, i * PANEL : (i + 1) * PANEL], axis=0, keepdims=True)
        row = (image[i : i + 1, :] - taken) / beta
        vector_out[2 * i : 2 * i + 1, :] = row[:, : PANEL // 2]
        vector_out[2 * i + 1 : 2 * i + 2, :] = row[:, PANEL // 2 :]
    values = jnp.sum(jnp.where(lane == sub, coef, zero), axis=0, keepdims=True)
    hessen_out[...] = jnp.where(lane[:1] == count, beta, values)


def call(kernel, specs, outs, scratch=()):
    shapes = [jax.ShapeDtypeStruct(shape, dtype) for shape, dtype in outs]
    return pl.pallas_call(
        kernel,
        out_shape=shapes,
        in_specs=specs,
        out_specs=[VMEM] * len(shapes),
        scratch_shapes=list(scratch),
        compiler_params=pltpu.CompilerParams(vmem_limit_bytes=24 << 20),
    )


def pinned(*arrays):
    return [pltpu.with_memory_space_constraint(a, pltpu.HBM) for a in arrays]


def like(array):
    return pltpu.VMEM(array.shape, array.dtype)


def body(
    basis, roots, near_blocks, near_ids, leaf_basis, far_coupling, far_ids, transfer, top_coupling, top_ids
):
    leaves, nears = near_blocks.shape[:2]
    fars, parents, tops = far_coupling.shape[1], *top_coupling.shape[:2]
    devices = lax.axis_size("grp") * lax.axis_size("leaf")
    mates = [(i, i ^ 1) for i in range(devices)]
    others = [(i, (((i + 1) ^ 1) - 1) % devices) for i in range(devices)]

    product, stack, basis, leaf_basis, transfer = call(
        start_kernel,
        [HBM] * 3,
        [((leaves, PANEL), F32), ((leaves, WIDTH), BF16)] + [(a.shape, a.dtype) for a in (basis, leaf_basis, transfer)],
        [pltpu.SemaphoreType.DMA((3,))],
    )(*pinned(basis, leaf_basis, transfer))
    far = lax.ppermute(stack, AXES, others)
    mate = lax.ppermute(stack, AXES, mates)
    roots = roots.reshape(1, -1)
    scales, crowded, near, slots, coupling, top, pick_slots, *picks = call(
        prepare_kernel,
        [VMEM] + [HBM] * 7,
        [
            ((roots.shape[1] * leaves, PANEL), F32),
            ((1, 128), jnp.int32),
            (near_blocks.shape, BF16),
            ((SLOTS + 1, PANEL, PANEL), BF16),
            ((fars * RANK, leaves * RANK), BF16),
            ((tops * PRANK, parents * PRANK), BF16),
            ((SLOTS * leaves, SOURCES), BF16),
            ((nears * leaves, SOURCES), BF16),
            ((fars * leaves, SOURCES), BF16),
            ((tops * leaves, SOURCES), BF16),
        ],
        [like(a) for a in (roots, near_blocks, far_coupling, top_coupling, near_ids, far_ids, top_ids)]
        + [pltpu.SMEM(near_ids.shape, near_ids.dtype), pltpu.VMEM(((SLOTS + 1) * leaves, 128), F32)]
        + [pltpu.SemaphoreType.DMA((7 + leaves,))],
    )(product, *pinned(roots, near_blocks, near_ids, far_coupling, far_ids, top_coupling, top_ids))
    matrices = (*picks, near, leaf_basis, coupling, transfer, top)
    partial = product
    steps = roots.shape[1] - 1
    outs = [((leaves, PANEL), F32), ((leaves, PANEL), F32), ((leaves, WIDTH), BF16)]
    early = [((leaves, PRANK), F32), ((leaves, leaves * RANK), F32), ((leaves, PANEL), F32)]
    packed = (crowded, pick_slots, slots)
    for step in range(steps):
        last = step == steps - 1
        state = (scales, product, partial, stack, mate)
        ready = call(functools.partial(step_early, step, last), [VMEM] * 13, early + outs)(*state, *matrices)
        product, partial, stack = call(functools.partial(step_late, step, last), [VMEM] * 23, outs)(
            *state, far, *packed, *matrices, *ready
        )
        far = lax.ppermute(stack, AXES, others)
        mate = lax.ppermute(stack, AXES, mates)
    state = (partial, stack, mate)
    ready = call(last_early, [VMEM] * 11, early + outs[:1])(*state, *matrices)
    image, sums = call(last_late, [VMEM] * 20, [outs[0], ((devices, 128), F32)])(
        *state, far, *packed, *matrices, *ready, basis
    )
    sums = lax.all_to_all(sums.reshape(devices, 1, 128), AXES, 0, 0, tiled=True)
    size = float(leaves * PANEL * devices)
    vector, hessen = call(
        functools.partial(finish_kernel, size), [VMEM] * 3, [((leaves * 2, 128), F32), ((1, 128), F32)]
    )(sums.reshape(devices, 128), image, basis)
    return vector.reshape(leaves * PANEL), hessen[0, : basis.shape[0] + 1]


def solution(mesh):
    split = P(AXES)
    in_specs = (P(None, AXES), P()) + (split,) * 8
    return jax.shard_map(body, mesh=mesh, in_specs=in_specs, out_specs=(split, P()), check_vma=False)
```

```python
import functools

import jax
import jax.numpy as jnp
from jax import lax
from jax.experimental import pallas as pl
from jax.experimental.pallas import tpu as pltpu
from jax.sharding import PartitionSpec as P

AXES = ("grp", "leaf")
F32 = jnp.float32
BF16 = jnp.bfloat16
NT = (((1,), (1,)), ((), ()))
VMEM = pl.BlockSpec(memory_space=pltpu.VMEM)
HBM = pl.BlockSpec(memory_space=pltpu.HBM)
PANEL, RANK, PRANK, WIDTH = 256, 64, 128, 512
T_AT, C_AT = PANEL, PANEL + PRANK
SOURCES = 32


def dot(a, b):
    return jnp.dot(a, b, preferred_element_type=F32)


def dot_nt(a, b):
    return lax.dot_general(a, b, NT, preferred_element_type=F32)


def diagonal(value, block):
    lane = lax.broadcasted_iota(jnp.int32, value.shape, 1)
    row = lax.broadcasted_iota(jnp.int32, value.shape, 0)
    return jnp.where(lane // block == row, value, jnp.zeros_like(value))


def flat(value):
    return jnp.broadcast_to(jnp.sum(value, axis=0, keepdims=True), value.shape)


def write_stack(field, leaf_basis, transfer, stack, turned=None):
    rounded = field.astype(BF16)
    stack[:, :PANEL] = rounded
    coeffs = dot(rounded, turned[...]) if turned is not None else dot_nt(rounded, leaf_basis)
    kept = diagonal(coeffs, RANK)
    folded = sum(kept[:, at : at + 2 * RANK] for at in range(0, kept.shape[1], 2 * RANK))
    coeffs = folded[:, :RANK] + folded[:, RANK:]
    stack[:, C_AT:] = jnp.concatenate([coeffs, jnp.zeros_like(coeffs)], axis=1).astype(BF16)
    spread = diagonal(flat(kept.astype(BF16).astype(F32)), 2 * RANK)
    stack[:, T_AT:C_AT] = dot(spread.astype(BF16), transfer).astype(BF16)


def tiles(value, rows):
    return jnp.concatenate([value[at : at + rows] for at in range(0, value.shape[0], rows)], axis=1)


def apply_rows(field, own, mate, far, pick_near, pick_far, pick_top, near, leaf_basis, coupling, transfer_turned, top):
    leaves = field.shape[0]
    rest = jnp.zeros((SOURCES - 3 * leaves, WIDTH), F32)
    window = jnp.concatenate(
        [own[...].astype(F32), mate[...].astype(F32), far[...].astype(F32), rest], axis=0
    ).astype(BF16)
    parents = tiles(dot(pick_top[...], window[:, T_AT:C_AT]), leaves).astype(BF16)
    coeffs = tiles(dot(pick_far[...], window[:, C_AT : C_AT + RANK]), leaves).astype(BF16)
    panels = dot(pick_near[...], window[:, :PANEL]).astype(BF16)
    tops = diagonal(dot(parents, top[...]), PRANK)
    tops = sum(tops[:, at : at + PRANK] for at in range(0, tops.shape[1], PRANK)).astype(BF16)
    local = diagonal(dot(coeffs, coupling[...]), RANK) + diagonal(dot(tops, transfer_turned[...]), 2 * RANK)
    total = dot(diagonal(flat(local), RANK).astype(BF16), leaf_basis)
    row = lax.broadcasted_iota(jnp.int32, total.shape, 0)
    for i in range(leaves):
        image = jnp.zeros(total.shape, F32)
        for k in range(near.shape[1]):
            image += dot(panels[k * leaves : (k + 1) * leaves], near[i, k])
        total += jnp.where(row == i, image, jnp.zeros_like(image))
    return 0.5 * field + total


def stacked(ref):
    return ref[...].reshape(ref.shape[0] * ref.shape[1], ref.shape[2])


def start_kernel(basis, leaf_basis, transfer, product, stack, basis_in, leaf_basis_in, transfer_in, sems):
    copies = [
        pltpu.make_async_copy(source, target, sems.at[n])
        for n, (source, target) in enumerate(
            ((basis, basis_in), (leaf_basis, leaf_basis_in), (transfer, transfer_in))
        )
    ]
    for copy in copies:
        copy.start()
    for copy in copies:
        copy.wait()
    count = basis.shape[0]
    for i in range(product.shape[0]):
        product[i : i + 1, :] = basis_in[count - 1 : count, i * PANEL : (i + 1) * PANEL]
    write_stack(product[...], stacked(leaf_basis_in), stacked(transfer_in), stack)


def identity(size):
    row = lax.broadcasted_iota(jnp.int32, (size, size), 0)
    return jnp.where(row == lax.broadcasted_iota(jnp.int32, (size, size), 1), 1.0, 0.0).astype(BF16)


def prepare_kernel(
    _, leaf_basis, transfer, roots, near, near_ids, coupling, far_ids, top, top_ids,
    scales, basis_turned, transfer_turned, near_out, coupling_out, top_out, pick_near, pick_far, pick_top,
    roots_in, near_in, coupling_in, top_in, near_ids_in, far_ids_in, top_ids_in, sems,
):
    leaves = near.shape[0]
    pairs = [
        (roots, roots_in), (near_ids, near_ids_in), (far_ids, far_ids_in), (top_ids, top_ids_in),
        (coupling, coupling_in), (top, top_in),
    ] + [(near.at[i], near_in.at[i]) for i in range(leaves)]
    copies = [
        pltpu.make_async_copy(source, target, sems.at[n]) for n, (source, target) in enumerate(pairs)
    ]
    for copy in copies:
        copy.start()
    basis_turned[...] = stacked(leaf_basis).T
    transfer_turned[...] = stacked(transfer).T
    unit = identity(PANEL)
    for copy in copies[:4]:
        copy.wait()
    for k in range(roots.shape[1]):
        scales[k * leaves : (k + 1) * leaves, :] = jnp.broadcast_to(
            roots_in[:, k : k + 1], (leaves, scales.shape[1])
        )
    place = lax.axis_index(AXES)
    odd = place % 2 == 1
    left, right = jnp.where(odd, leaves, 2 * leaves), jnp.where(odd, 2 * leaves, leaves)
    for ids_in, pick, rows in (
        (near_ids_in, pick_near, leaves), (far_ids_in, pick_far, leaves), (top_ids_in, pick_top, leaves // 2),
    ):
        away = ids_in[...] - place * rows
        where = jnp.where(away < 0, away + rows + left, jnp.where(away < rows, away, away - rows + right))
        lane = lax.broadcasted_iota(jnp.int32, (rows, SOURCES), 1)
        for k in range(ids_in.shape[1]):
            hot = jnp.where(lane == where[:, k : k + 1], 1.0, 0.0)
            if rows < leaves:
                hot = jnp.concatenate([hot, jnp.zeros((leaves - rows, SOURCES), F32)], axis=0)
            pick[k * leaves : (k + 1) * leaves, :] = hot.astype(BF16)
    copies[4].wait()
    for k in range(coupling.shape[1]):
        rows = jnp.concatenate([coupling_in[i, k] for i in range(leaves)], axis=0)
        coupling_out[k * RANK : (k + 1) * RANK, :] = rows.T
    copies[5].wait()
    for p in range(top.shape[0]):
        for k in range(top.shape[1]):
            rows, lanes = slice(k * PRANK, (k + 1) * PRANK), slice(p * PRANK, (p + 1) * PRANK)
            top_out[rows, lanes] = top_in[p, k].T
    for i in range(leaves):
        copies[6 + i].wait()
        for k in range(near.shape[1]):
            near_out[i, k] = dot_nt(unit, near_in[i, k]).astype(BF16) if k % 2 else near_in[i, k].T


def at_an_end():
    place = lax.axis_index(AXES)
    return jnp.logical_or(place == 0, place == lax.axis_size(AXES) - 1)


def advance(step, last, image, field, scales, partial, matrices, outs):
    leaves = field.shape[0]
    root = scales[step * leaves : (step + 1) * leaves, :]
    after = field - image / root
    total = field / root
    if step:
        total += partial[...]
    if last:
        total += after / scales[(step + 1) * leaves : (step + 2) * leaves, :]
    else:
        outs[2][...] = after
    outs[0][...] = total
    write_stack(total if last else after, stacked(matrices[1]), stacked(matrices[3]), outs[1], matrices[5])


def image_of(field, own, mate, far, picks, matrices):
    near, leaf_basis, coupling, _, top, _, transfer_turned = matrices
    return apply_rows(
        field, own, mate, far, *picks, near, stacked(leaf_basis), coupling, transfer_turned, top
    )


def step_early(step, last, scales, product, partial, own, mate, *rest):
    picks, matrices, outs = rest[:3], rest[3:10], rest[10:]

    @pl.when(at_an_end())
    def _():
        field = product[...]
        image = image_of(field, own, mate, own, picks, matrices)
        advance(step, last, image, field, scales, partial, matrices, outs)


def step_late(step, last, scales, product, partial, own, mate, far, *rest):
    picks, matrices, rest = rest[:3], rest[3:10], rest[10:]
    ready, outs = rest[: len(rest) // 2], rest[len(rest) // 2 :]
    end = at_an_end()

    @pl.when(jnp.logical_not(end))
    def _():
        field = product[...]
        image = image_of(field, own, mate, far, picks, matrices)
        advance(step, last, image, field, scales, partial, matrices, outs)

    @pl.when(end)
    def _():
        for source, target in zip(ready, outs):
            target[...] = source[...]


def pack_iota(count):
    lane = lax.broadcasted_iota(jnp.int32, (count, 128), 1)
    return lane, lax.broadcasted_iota(jnp.int32, (count, 128), 0)


def last_early(field, own, mate, *rest):
    picks, matrices, (basis, image_out, gram) = rest[:3], rest[3:10], rest[10:]
    count = basis.shape[0]
    lane, sub = pack_iota(count)
    vectors = basis[...]
    packed = jnp.zeros((count, 128), F32)
    for n in range(count):
        column = jnp.sum(vectors * vectors[n : n + 1], axis=1, keepdims=True)
        packed = jnp.where(lane == n * count + sub, column, packed)
    gram[...] = packed

    @pl.when(at_an_end())
    def _():
        image_out[...] = image_of(field[...], own, mate, own, picks, matrices)


def last_late(field, own, mate, far, *rest):
    picks, matrices, (basis, ready, gram, image_out, sums) = rest[:3], rest[3:10], rest[10:]
    end = at_an_end()

    @pl.when(jnp.logical_not(end))
    def _():
        image_out[...] = image_of(field[...], own, mate, far, picks, matrices)

    @pl.when(end)
    def _():
        image_out[...] = ready[...]

    image = image_out[...]
    count, leaves = basis.shape[0], image.shape[0]
    lane, sub = pack_iota(count)
    packed = gram[...]
    dots = jnp.zeros((count, PANEL), F32)
    for i in range(leaves):
        dots += basis[:, i * PANEL : (i + 1) * PANEL] * image[i : i + 1]
    column = jnp.sum(dots, axis=1, keepdims=True)
    packed = jnp.where(lane == count * count + sub, column, packed)
    column = jnp.sum(image * image, axis=1, keepdims=True)
    packed = jnp.where(lane == count * count + count, column, packed)
    sums[...] = jnp.broadcast_to(jnp.sum(packed, axis=0, keepdims=True), sums.shape)


def finish_kernel(size, sums, image, basis, vector_out, hessen_out):
    count, leaves = basis.shape[0], image.shape[0]
    lane = lax.broadcasted_iota(jnp.int32, (count, 128), 1)
    sub = lax.broadcasted_iota(jnp.int32, (count, 128), 0)
    totals = jnp.broadcast_to(jnp.sum(sums[...], axis=0, keepdims=True) / size, (count, 128))
    zero = jnp.zeros((count, 128), F32)
    here = lane == count * count + sub
    coef = jnp.sum(jnp.where(here, totals, zero), axis=1, keepdims=True)
    inner = jnp.sum(jnp.where(lane % count == sub, coef, zero), axis=0, keepdims=True)
    outer = jnp.sum(jnp.where(lane // count == sub, coef, zero), axis=0, keepdims=True)
    gram = jnp.where(lane[:1] < count * count, totals[:1] * inner * outer, zero[:1])
    length = jnp.where(lane[:1] == count * count + count, totals[:1], zero[:1])
    squared = jnp.sum(gram + length, axis=1, keepdims=True)
    squared = squared - 2.0 * jnp.sum(coef * coef, axis=0, keepdims=True)
    beta = jnp.sqrt(squared + 1e-06)
    for i in range(leaves):
        taken = jnp.sum(coef * basis[:, i * PANEL : (i + 1) * PANEL], axis=0, keepdims=True)
        row = (image[i : i + 1, :] - taken) / beta
        vector_out[2 * i : 2 * i + 1, :] = row[:, : PANEL // 2]
        vector_out[2 * i + 1 : 2 * i + 2, :] = row[:, PANEL // 2 :]
    values = jnp.sum(jnp.where(lane == sub, coef, zero), axis=0, keepdims=True)
    hessen_out[...] = jnp.where(lane[:1] == count, beta, values)[0, : count + 1]


def call(kernel, specs, outs, scratch=()):
    shapes = [jax.ShapeDtypeStruct(shape, dtype) for shape, dtype in outs]
    return pl.pallas_call(
        kernel,
        out_shape=shapes,
        in_specs=specs,
        out_specs=[VMEM] * len(shapes),
        scratch_shapes=list(scratch),
        compiler_params=pltpu.CompilerParams(vmem_limit_bytes=24 << 20),
    )


def pinned(*arrays):
    return [pltpu.with_memory_space_constraint(a, pltpu.HBM) for a in arrays]


def like(array):
    return pltpu.VMEM(array.shape, array.dtype)


def body(
    basis, roots, near_blocks, near_ids, leaf_basis, far_coupling, far_ids, transfer, top_coupling, top_ids
):
    leaves, nears = near_blocks.shape[:2]
    fars, parents, tops = far_coupling.shape[1], *top_coupling.shape[:2]
    devices = lax.axis_size("grp") * lax.axis_size("leaf")
    mates = [(i, i ^ 1) for i in range(devices)]
    others = [(i, (((i + 1) ^ 1) - 1) % devices) for i in range(devices)]

    product, stack, basis, leaf_basis, transfer = call(
        start_kernel,
        [HBM] * 3,
        [((leaves, PANEL), F32), ((leaves, WIDTH), BF16)] + [(a.shape, a.dtype) for a in (basis, leaf_basis, transfer)],
        [pltpu.SemaphoreType.DMA((3,))],
    )(*pinned(basis, leaf_basis, transfer))
    far = lax.ppermute(stack, AXES, others)
    mate = lax.ppermute(stack, AXES, mates)
    roots = roots.reshape(1, -1)
    scales, basis_turned, transfer_turned, near, coupling, top, *picks = call(
        prepare_kernel,
        [VMEM] * 3 + [HBM] * 7,
        [
            ((roots.shape[1] * leaves, PANEL), F32),
            ((PANEL, leaves * RANK), BF16),
            ((PRANK, leaves * RANK), BF16),
            (near_blocks.shape, BF16),
            ((fars * RANK, leaves * RANK), BF16),
            ((tops * PRANK, parents * PRANK), BF16),
            ((nears * leaves, SOURCES), BF16),
            ((fars * leaves, SOURCES), BF16),
            ((tops * leaves, SOURCES), BF16),
        ],
        [like(a) for a in (roots, near_blocks, far_coupling, top_coupling, near_ids, far_ids, top_ids)]
        + [pltpu.SemaphoreType.DMA((6 + leaves,))],
    )(product, leaf_basis, transfer, *pinned(roots, near_blocks, near_ids, far_coupling, far_ids, top_coupling, top_ids))
    matrices = (*picks, near, leaf_basis, coupling, transfer, top, basis_turned, transfer_turned)
    partial = product
    steps = roots.shape[1] - 1
    square = ((leaves, PANEL), F32)
    for step in range(steps):
        last = step == steps - 1
        outs = [square, ((leaves, WIDTH), BF16)] + ([] if last else [square])
        state = (scales, product, partial, stack, mate)
        ready = call(functools.partial(step_early, step, last), [VMEM] * 15, outs)(*state, *matrices)
        partial, stack, *after = call(
            functools.partial(step_late, step, last), [VMEM] * (16 + len(outs)), outs
        )(*state, far, *matrices, *ready)
        product = None if last else after[0]
        far = lax.ppermute(stack, AXES, others)
        mate = lax.ppermute(stack, AXES, mates)
    state = (partial, stack, mate)
    ready = call(last_early, [VMEM] * 14, [square, ((basis.shape[0], 128), F32)])(*state, *matrices, basis)
    image, sums = call(last_late, [VMEM] * 17, [square, ((devices, 128), F32)])(
        *state, far, *matrices, basis, *ready
    )
    sums = lax.all_to_all(sums.reshape(devices, 1, 128), AXES, 0, 0, tiled=True)
    size = float(leaves * PANEL * devices)
    vector, hessen = call(
        functools.partial(finish_kernel, size), [VMEM] * 3, [((leaves * 2, 128), F32), ((basis.shape[0] + 1,), F32)]
    )(sums.reshape(devices, 128), image, basis)
    return vector.reshape(leaves * PANEL), hessen


def solution(mesh):
    split = P(AXES)
    in_specs = (P(None, AXES), P()) + (split,) * 8
    return jax.shard_map(body, mesh=mesh, in_specs=in_specs, out_specs=(split, P()), check_vma=False)
```

```python
import functools

import jax
import jax.numpy as jnp
from jax import lax
from jax.experimental import pallas as pl
from jax.experimental.pallas import tpu as pltpu
from jax.sharding import PartitionSpec as P

AXES = ("grp", "leaf")
F32 = jnp.float32
BF16 = jnp.bfloat16
NT = (((1,), (1,)), ((), ()))
VMEM = pl.BlockSpec(memory_space=pltpu.VMEM)
HBM = pl.BlockSpec(memory_space=pltpu.HBM)
PANEL, RANK, PRANK, WIDTH = 256, 64, 128, 512
T_AT, C_AT = PANEL, PANEL + PRANK
SOURCES = 32


def dot(a, b):
    return jnp.dot(a, b, preferred_element_type=F32)


def dot_nt(a, b):
    return lax.dot_general(a, b, NT, preferred_element_type=F32)


def diagonal(value, block):
    lane = lax.broadcasted_iota(jnp.int32, value.shape, 1)
    row = lax.broadcasted_iota(jnp.int32, value.shape, 0)
    return jnp.where(lane // block == row, value, jnp.zeros_like(value))


def flat(value):
    return jnp.broadcast_to(jnp.sum(value, axis=0, keepdims=True), value.shape)


def write_stack(field, leaf_basis, transfer, stack, turned=None):
    rounded = field.astype(BF16)
    stack[:, :PANEL] = rounded
    coeffs = dot(rounded, turned[...]) if turned is not None else dot_nt(rounded, leaf_basis)
    kept = diagonal(coeffs, RANK)
    folded = sum(kept[:, at : at + 2 * RANK] for at in range(0, kept.shape[1], 2 * RANK))
    coeffs = folded[:, :RANK] + folded[:, RANK:]
    stack[:, C_AT:] = jnp.concatenate([coeffs, jnp.zeros_like(coeffs)], axis=1).astype(BF16)
    spread = diagonal(flat(kept.astype(BF16).astype(F32)), 2 * RANK)
    stack[:, T_AT:C_AT] = dot(spread.astype(BF16), transfer).astype(BF16)


def tiles(value, rows):
    return jnp.concatenate([value[at : at + rows] for at in range(0, value.shape[0], rows)], axis=1)


def apply_rows(field, own, mate, far, pick_near, pick_far, pick_top, near, leaf_basis, coupling, transfer_turned, top):
    leaves = field.shape[0]
    rest = jnp.zeros((SOURCES - 3 * leaves, WIDTH), F32)
    window = jnp.concatenate(
        [own[...].astype(F32), mate[...].astype(F32), far[...].astype(F32), rest], axis=0
    ).astype(BF16)
    panels = dot(pick_near[...], window[:, :PANEL]).astype(BF16)
    parents = tiles(dot(pick_top[...], window[:, T_AT:C_AT]), leaves).astype(BF16)
    coeffs = tiles(dot(pick_far[...], window[:, C_AT : C_AT + RANK]), leaves).astype(BF16)
    row = lax.broadcasted_iota(jnp.int32, field.shape, 0)

    def near_rows(total, some):
        for i in some:
            image = jnp.zeros(total.shape, F32)
            for k in range(near.shape[1]):
                image += dot(panels[k * leaves : (k + 1) * leaves], near[i, k])
            total += jnp.where(row == i, image, jnp.zeros_like(image))
        return total

    quarter = leaves // 4
    total = near_rows(0.5 * field, range(quarter))
    tops = diagonal(dot(parents, top[...]), PRANK)
    local = diagonal(dot(coeffs, coupling[...]), RANK)
    total = near_rows(total, range(quarter, 2 * quarter))
    tops = sum(tops[:, at : at + PRANK] for at in range(0, tops.shape[1], PRANK)).astype(BF16)
    local += diagonal(dot(tops, transfer_turned[...]), 2 * RANK)
    total = near_rows(total, range(2 * quarter, 3 * quarter))
    rows = dot(diagonal(flat(local), RANK).astype(BF16), leaf_basis)
    total = near_rows(total, range(3 * quarter, leaves))
    return total + rows


def stacked(ref):
    return ref[...].reshape(ref.shape[0] * ref.shape[1], ref.shape[2])


def start_kernel(basis, leaf_basis, transfer, product, stack, basis_in, leaf_basis_in, transfer_in, sems):
    copies = [
        pltpu.make_async_copy(source, target, sems.at[n])
        for n, (source, target) in enumerate(
            ((basis, basis_in), (leaf_basis, leaf_basis_in), (transfer, transfer_in))
        )
    ]
    for copy in copies:
        copy.start()
    for copy in copies:
        copy.wait()
    count = basis.shape[0]
    for i in range(product.shape[0]):
        product[i : i + 1, :] = basis_in[count - 1 : count, i * PANEL : (i + 1) * PANEL]
    write_stack(product[...], stacked(leaf_basis_in), stacked(transfer_in), stack)


def identity(size):
    row = lax.broadcasted_iota(jnp.int32, (size, size), 0)
    return jnp.where(row == lax.broadcasted_iota(jnp.int32, (size, size), 1), 1.0, 0.0).astype(BF16)


def prepare_kernel(
    _, leaf_basis, transfer, roots, near, near_ids, coupling, far_ids, top, top_ids,
    scales, basis_turned, transfer_turned, near_out, coupling_out, top_out, pick_near, pick_far, pick_top,
    roots_in, near_in, coupling_in, top_in, near_ids_in, far_ids_in, top_ids_in, sems,
):
    leaves = near.shape[0]
    pairs = [
        (roots, roots_in), (near_ids, near_ids_in), (far_ids, far_ids_in), (top_ids, top_ids_in),
        (coupling, coupling_in), (top, top_in),
    ] + [(near.at[i], near_in.at[i]) for i in range(leaves)]
    copies = [
        pltpu.make_async_copy(source, target, sems.at[n]) for n, (source, target) in enumerate(pairs)
    ]
    for copy in copies:
        copy.start()
    basis_turned[...] = stacked(leaf_basis).T
    transfer_turned[...] = stacked(transfer).T
    unit = identity(PANEL)
    for copy in copies[:4]:
        copy.wait()
    for k in range(roots.shape[1]):
        scales[k * leaves : (k + 1) * leaves, :] = jnp.broadcast_to(
            1.0 / roots_in[:, k : k + 1], (leaves, scales.shape[1])
        )
    place = lax.axis_index(AXES)
    odd = place % 2 == 1
    left, right = jnp.where(odd, leaves, 2 * leaves), jnp.where(odd, 2 * leaves, leaves)
    for ids_in, pick, rows in (
        (near_ids_in, pick_near, leaves), (far_ids_in, pick_far, leaves), (top_ids_in, pick_top, leaves // 2),
    ):
        away = ids_in[...] - place * rows
        where = jnp.where(away < 0, away + rows + left, jnp.where(away < rows, away, away - rows + right))
        lane = lax.broadcasted_iota(jnp.int32, (rows, SOURCES), 1)
        for k in range(ids_in.shape[1]):
            hot = jnp.where(lane == where[:, k : k + 1], 1.0, 0.0)
            if rows < leaves:
                hot = jnp.concatenate([hot, jnp.zeros((leaves - rows, SOURCES), F32)], axis=0)
            pick[k * leaves : (k + 1) * leaves, :] = hot.astype(BF16)
    copies[4].wait()
    for k in range(coupling.shape[1]):
        rows = jnp.concatenate([coupling_in[i, k] for i in range(leaves)], axis=0)
        coupling_out[k * RANK : (k + 1) * RANK, :] = rows.T
    copies[5].wait()
    for p in range(top.shape[0]):
        for k in range(top.shape[1]):
            rows, lanes = slice(k * PRANK, (k + 1) * PRANK), slice(p * PRANK, (p + 1) * PRANK)
            top_out[rows, lanes] = top_in[p, k].T
    for i in range(leaves):
        copies[6 + i].wait()
        for k in range(near.shape[1]):
            near_out[i, k] = dot_nt(unit, near_in[i, k]).astype(BF16) if k % 2 else near_in[i, k].T


def at_an_end():
    place = lax.axis_index(AXES)
    return jnp.logical_or(place == 0, place == lax.axis_size(AXES) - 1)


def advance(step, last, image, field, scales, partial, matrices, outs):
    leaves = field.shape[0]
    root = scales[step * leaves : (step + 1) * leaves, :]
    after = field - image * root
    total = field * root
    if step:
        total += partial[...]
    if last:
        total += after * scales[(step + 1) * leaves : (step + 2) * leaves, :]
    else:
        outs[2][...] = after
    outs[0][...] = total
    write_stack(total if last else after, stacked(matrices[1]), stacked(matrices[3]), outs[1], matrices[5])


def image_of(field, own, mate, far, picks, matrices):
    near, leaf_basis, coupling, _, top, _, transfer_turned = matrices
    return apply_rows(
        field, own, mate, far, *picks, near, stacked(leaf_basis), coupling, transfer_turned, top
    )


def step_early(step, last, scales, product, partial, own, mate, *rest):
    picks, matrices, outs = rest[:3], rest[3:10], rest[10:]

    @pl.when(at_an_end())
    def _():
        field = product[...]
        image = image_of(field, own, mate, own, picks, matrices)
        advance(step, last, image, field, scales, partial, matrices, outs)


def step_late(step, last, scales, product, partial, own, mate, far, *rest):
    picks, matrices, rest = rest[:3], rest[3:10], rest[10:]
    ready, outs = rest[: len(rest) // 2], rest[len(rest) // 2 :]
    end = at_an_end()

    @pl.when(jnp.logical_not(end))
    def _():
        field = product[...]
        image = image_of(field, own, mate, far, picks, matrices)
        advance(step, last, image, field, scales, partial, matrices, outs)

    @pl.when(end)
    def _():
        for source, target in zip(ready, outs):
            target[...] = source[...]


def pack_iota(count):
    lane = lax.broadcasted_iota(jnp.int32, (count, 128), 1)
    return lane, lax.broadcasted_iota(jnp.int32, (count, 128), 0)


def last_early(field, own, mate, *rest):
    picks, matrices, (basis, image_out, gram) = rest[:3], rest[3:10], rest[10:]
    count = basis.shape[0]
    lane, sub = pack_iota(count)
    vectors = basis[...]
    packed = jnp.zeros((count, 128), F32)
    for n in range(count):
        column = jnp.sum(vectors * vectors[n : n + 1], axis=1, keepdims=True)
        packed = jnp.where(lane == n * count + sub, column, packed)
    gram[...] = packed

    @pl.when(at_an_end())
    def _():
        image_out[...] = image_of(field[...], own, mate, own, picks, matrices)


def last_late(field, own, mate, far, *rest):
    picks, matrices, (basis, ready, gram, image_out, sums) = rest[:3], rest[3:10], rest[10:]
    end = at_an_end()

    @pl.when(jnp.logical_not(end))
    def _():
        image_out[...] = image_of(field[...], own, mate, far, picks, matrices)

    @pl.when(end)
    def _():
        image_out[...] = ready[...]

    image = image_out[...]
    count, leaves = basis.shape[0], image.shape[0]
    lane, sub = pack_iota(count)
    packed = gram[...]
    dots = jnp.zeros((count, PANEL), F32)
    for i in range(leaves):
        dots += basis[:, i * PANEL : (i + 1) * PANEL] * image[i : i + 1]
    column = jnp.sum(dots, axis=1, keepdims=True)
    packed = jnp.where(lane == count * count + sub, column, packed)
    column = jnp.sum(image * image, axis=1, keepdims=True)
    packed = jnp.where(lane == count * count + count, column, packed)
    sums[...] = jnp.broadcast_to(jnp.sum(packed, axis=0, keepdims=True), sums.shape)


def finish_kernel(size, sums, image, basis, vector_out, hessen_out):
    count, leaves = basis.shape[0], image.shape[0]
    lane = lax.broadcasted_iota(jnp.int32, (count, 128), 1)
    sub = lax.broadcasted_iota(jnp.int32, (count, 128), 0)
    totals = jnp.broadcast_to(jnp.sum(sums[...], axis=0, keepdims=True) / size, (count, 128))
    zero = jnp.zeros((count, 128), F32)
    here = lane == count * count + sub
    coef = jnp.sum(jnp.where(here, totals, zero), axis=1, keepdims=True)
    inner = jnp.sum(jnp.where(lane % count == sub, coef, zero), axis=0, keepdims=True)
    outer = jnp.sum(jnp.where(lane // count == sub, coef, zero), axis=0, keepdims=True)
    gram = jnp.where(lane[:1] < count * count, totals[:1] * inner * outer, zero[:1])
    length = jnp.where(lane[:1] == count * count + count, totals[:1], zero[:1])
    squared = jnp.sum(gram + length, axis=1, keepdims=True)
    squared = squared - 2.0 * jnp.sum(coef * coef, axis=0, keepdims=True)
    beta = jnp.sqrt(squared + 1e-06)
    for i in range(leaves):
        taken = jnp.sum(coef * basis[:, i * PANEL : (i + 1) * PANEL], axis=0, keepdims=True)
        row = (image[i : i + 1, :] - taken) / beta
        vector_out[2 * i : 2 * i + 1, :] = row[:, : PANEL // 2]
        vector_out[2 * i + 1 : 2 * i + 2, :] = row[:, PANEL // 2 :]
    values = jnp.sum(jnp.where(lane == sub, coef, zero), axis=0, keepdims=True)
    hessen_out[...] = jnp.where(lane[:1] == count, beta, values)[0, : count + 1]


def call(kernel, specs, outs, scratch=()):
    shapes = [jax.ShapeDtypeStruct(shape, dtype) for shape, dtype in outs]
    return pl.pallas_call(
        kernel,
        out_shape=shapes,
        in_specs=specs,
        out_specs=[VMEM] * len(shapes),
        scratch_shapes=list(scratch),
        compiler_params=pltpu.CompilerParams(vmem_limit_bytes=24 << 20),
    )


def pinned(*arrays):
    return [pltpu.with_memory_space_constraint(a, pltpu.HBM) for a in arrays]


def like(array):
    return pltpu.VMEM(array.shape, array.dtype)


def body(
    basis, roots, near_blocks, near_ids, leaf_basis, far_coupling, far_ids, transfer, top_coupling, top_ids
):
    leaves, nears = near_blocks.shape[:2]
    fars, parents, tops = far_coupling.shape[1], *top_coupling.shape[:2]
    devices = lax.axis_size("grp") * lax.axis_size("leaf")
    mates = [(i, i ^ 1) for i in range(devices)]
    others = [(i, (((i + 1) ^ 1) - 1) % devices) for i in range(devices)]

    product, stack, basis, leaf_basis, transfer = call(
        start_kernel,
        [HBM] * 3,
        [((leaves, PANEL), F32), ((leaves, WIDTH), BF16)] + [(a.shape, a.dtype) for a in (basis, leaf_basis, transfer)],
        [pltpu.SemaphoreType.DMA((3,))],
    )(*pinned(basis, leaf_basis, transfer))
    far = lax.ppermute(stack, AXES, others)
    mate = lax.ppermute(stack, AXES, mates)
    mate, far = lax.optimization_barrier((mate, far))
    roots = roots.reshape(1, -1)
    scales, basis_turned, transfer_turned, near, coupling, top, *picks = call(
        prepare_kernel,
        [VMEM] * 3 + [HBM] * 7,
        [
            ((roots.shape[1] * leaves, PANEL), F32),
            ((PANEL, leaves * RANK), BF16),
            ((PRANK, leaves * RANK), BF16),
            (near_blocks.shape, BF16),
            ((fars * RANK, leaves * RANK), BF16),
            ((tops * PRANK, parents * PRANK), BF16),
            ((nears * leaves, SOURCES), BF16),
            ((fars * leaves, SOURCES), BF16),
            ((tops * leaves, SOURCES), BF16),
        ],
        [like(a) for a in (roots, near_blocks, far_coupling, top_coupling, near_ids, far_ids, top_ids)]
        + [pltpu.SemaphoreType.DMA((6 + leaves,))],
    )(product, leaf_basis, transfer, *pinned(roots, near_blocks, near_ids, far_coupling, far_ids, top_coupling, top_ids))
    matrices = (*picks, near, leaf_basis, coupling, transfer, top, basis_turned, transfer_turned)
    partial = product
    steps = roots.shape[1] - 1
    square = ((leaves, PANEL), F32)
    for step in range(steps):
        last = step == steps - 1
        outs = [square, ((leaves, WIDTH), BF16)] + ([] if last else [square])
        state = (scales, product, partial, stack, mate)
        ready = call(functools.partial(step_early, step, last), [VMEM] * 15, outs)(*state, *matrices)
        partial, stack, *after = call(
            functools.partial(step_late, step, last), [VMEM] * (16 + len(outs)), outs
        )(*state, far, *matrices, *ready)
        product = None if last else after[0]
        far = lax.ppermute(stack, AXES, others)
        mate = lax.ppermute(stack, AXES, mates)
    state = (partial, stack, mate)
    ready = call(last_early, [VMEM] * 14, [square, ((basis.shape[0], 128), F32)])(*state, *matrices, basis)
    image, sums = call(last_late, [VMEM] * 17, [square, ((devices, 128), F32)])(
        *state, far, *matrices, basis, *ready
    )
    sums = lax.all_to_all(sums.reshape(devices, 1, 128), AXES, 0, 0, tiled=True)
    size = float(leaves * PANEL * devices)
    vector, hessen = call(
        functools.partial(finish_kernel, size), [VMEM] * 3, [((leaves * 2, 128), F32), ((basis.shape[0] + 1,), F32)]
    )(sums.reshape(devices, 128), image, basis)
    return vector.reshape(leaves * PANEL), hessen


def solution(mesh):
    split = P(AXES)
    in_specs = (P(None, AXES), P()) + (split,) * 8
    return jax.shard_map(body, mesh=mesh, in_specs=in_specs, out_specs=(split, P()), check_vma=False)
```

```python
import functools

import jax
import jax.numpy as jnp
from jax import lax
from jax.experimental import pallas as pl
from jax.experimental.pallas import tpu as pltpu
from jax.sharding import PartitionSpec as P

AXES = ("grp", "leaf")
F32 = jnp.float32
BF16 = jnp.bfloat16
NT = (((1,), (1,)), ((), ()))
VMEM = pl.BlockSpec(memory_space=pltpu.VMEM)
HBM = pl.BlockSpec(memory_space=pltpu.HBM)
PANEL, RANK, PRANK, WIDTH = 256, 64, 128, 512
T_AT, C_AT = PANEL, PANEL + PRANK
SOURCES = 32


def dot(a, b):
    return jnp.dot(a, b, preferred_element_type=F32)


def dot_nt(a, b):
    return lax.dot_general(a, b, NT, preferred_element_type=F32)


def diagonal(value, block):
    lane = lax.broadcasted_iota(jnp.int32, value.shape, 1)
    row = lax.broadcasted_iota(jnp.int32, value.shape, 0)
    return jnp.where(lane // block == row, value, jnp.zeros_like(value))


def flat(value):
    return jnp.broadcast_to(jnp.sum(value, axis=0, keepdims=True), value.shape)


def write_stack(field, leaf_basis, transfer, stack, turned=None):
    rounded = field.astype(BF16)
    stack[:, :PANEL] = rounded
    coeffs = dot(rounded, turned[...]) if turned is not None else dot_nt(rounded, leaf_basis)
    kept = diagonal(coeffs, RANK)
    folded = sum(kept[:, at : at + 2 * RANK] for at in range(0, kept.shape[1], 2 * RANK))
    coeffs = folded[:, :RANK] + folded[:, RANK:]
    stack[:, C_AT:] = jnp.concatenate([coeffs, jnp.zeros_like(coeffs)], axis=1).astype(BF16)
    spread = diagonal(flat(kept.astype(BF16).astype(F32)), 2 * RANK)
    stack[:, T_AT:C_AT] = dot(spread.astype(BF16), transfer).astype(BF16)


def tiles(value, rows):
    return jnp.concatenate([value[at : at + rows] for at in range(0, value.shape[0], rows)], axis=1)


def apply_rows(field, own, mate, far, pick_near, pick_far, pick_top, near, leaf_basis, coupling, transfer_turned, top):
    leaves = field.shape[0]
    rest = jnp.zeros((SOURCES - 3 * leaves, WIDTH), F32)
    window = jnp.concatenate(
        [own[...].astype(F32), mate[...].astype(F32), far[...].astype(F32), rest], axis=0
    ).astype(BF16)
    panels = dot(pick_near[...], window[:, :PANEL]).astype(BF16)
    parents = tiles(dot(pick_top[...], window[:, T_AT:C_AT]), leaves).astype(BF16)
    coeffs = tiles(dot(pick_far[...], window[:, C_AT : C_AT + RANK]), leaves).astype(BF16)
    row = lax.broadcasted_iota(jnp.int32, field.shape, 0)

    def near_rows(total, some):
        for i in some:
            image = jnp.zeros(total.shape, F32)
            for k in range(near.shape[1]):
                image += dot(panels[k * leaves : (k + 1) * leaves], near[i, k])
            total += jnp.where(row == i, image, jnp.zeros_like(image))
        return total

    quarter = leaves // 4
    total = near_rows(0.5 * field, range(2 * quarter))
    tops = diagonal(dot(parents, top[...]), PRANK)
    local = diagonal(dot(coeffs, coupling[...]), RANK)
    total = near_rows(total, range(2 * quarter, 3 * quarter))
    tops = sum(tops[:, at : at + PRANK] for at in range(0, tops.shape[1], PRANK)).astype(BF16)
    local += diagonal(dot(tops, transfer_turned[...]), 2 * RANK)
    total = near_rows(total, range(3 * quarter, leaves))
    rows = dot(diagonal(flat(local), RANK).astype(BF16), leaf_basis)
    return total + rows


def stacked(ref):
    return ref[...].reshape(ref.shape[0] * ref.shape[1], ref.shape[2])


def start_kernel(basis, leaf_basis, transfer, product, stack, basis_in, leaf_basis_in, transfer_in, sems):
    copies = [
        pltpu.make_async_copy(source, target, sems.at[n])
        for n, (source, target) in enumerate(
            ((basis, basis_in), (leaf_basis, leaf_basis_in), (transfer, transfer_in))
        )
    ]
    for copy in copies:
        copy.start()
    for copy in copies:
        copy.wait()
    count = basis.shape[0]
    for i in range(product.shape[0]):
        product[i : i + 1, :] = basis_in[count - 1 : count, i * PANEL : (i + 1) * PANEL]
    write_stack(product[...], stacked(leaf_basis_in), stacked(transfer_in), stack)


def identity(size):
    row = lax.broadcasted_iota(jnp.int32, (size, size), 0)
    return jnp.where(row == lax.broadcasted_iota(jnp.int32, (size, size), 1), 1.0, 0.0).astype(BF16)


def prepare_kernel(
    _, leaf_basis, transfer, roots, near, near_ids, coupling, far_ids, top, top_ids,
    scales, basis_turned, transfer_turned, near_out, coupling_out, top_out, pick_near, pick_far, pick_top,
    roots_in, near_in, coupling_in, top_in, near_ids_in, far_ids_in, top_ids_in, sems,
):
    leaves = near.shape[0]
    pairs = [
        (roots, roots_in), (near_ids, near_ids_in), (far_ids, far_ids_in), (top_ids, top_ids_in),
        (coupling, coupling_in), (top, top_in),
    ] + [(near.at[i], near_in.at[i]) for i in range(leaves)]
    copies = [
        pltpu.make_async_copy(source, target, sems.at[n]) for n, (source, target) in enumerate(pairs)
    ]
    for copy in copies:
        copy.start()
    basis_turned[...] = stacked(leaf_basis).T
    transfer_turned[...] = stacked(transfer).T
    unit = identity(PANEL)
    for copy in copies[:6]:
        copy.wait()
    for k in range(roots.shape[1]):
        scales[k * leaves : (k + 1) * leaves, :] = jnp.broadcast_to(
            1.0 / roots_in[:, k : k + 1], (leaves, scales.shape[1])
        )
    place = lax.axis_index(AXES)
    odd = place % 2 == 1
    left, right = jnp.where(odd, leaves, 2 * leaves), jnp.where(odd, 2 * leaves, leaves)
    for ids_in, pick, rows in (
        (near_ids_in, pick_near, leaves), (far_ids_in, pick_far, leaves), (top_ids_in, pick_top, leaves // 2),
    ):
        away = ids_in[...] - place * rows
        where = jnp.where(away < 0, away + rows + left, jnp.where(away < rows, away, away - rows + right))
        lane = lax.broadcasted_iota(jnp.int32, (rows, SOURCES), 1)
        for k in range(ids_in.shape[1]):
            hot = jnp.where(lane == where[:, k : k + 1], 1.0, 0.0)
            if rows < leaves:
                hot = jnp.concatenate([hot, jnp.zeros((leaves - rows, SOURCES), F32)], axis=0)
            pick[k * leaves : (k + 1) * leaves, :] = hot.astype(BF16)
    for k in range(coupling.shape[1]):
        rows = jnp.concatenate([coupling_in[i, k] for i in range(leaves)], axis=0)
        coupling_out[k * RANK : (k + 1) * RANK, :] = rows.T
    for p in range(top.shape[0]):
        for k in range(top.shape[1]):
            rows, lanes = slice(k * PRANK, (k + 1) * PRANK), slice(p * PRANK, (p + 1) * PRANK)
            top_out[rows, lanes] = top_in[p, k].T
    for i in range(leaves):
        for copy in copies[6 + i : 8 + i] if i % 2 == 0 else ():
            copy.wait()
        for k in range(near.shape[1]):
            near_out[i, k] = dot_nt(unit, near_in[i, k]).astype(BF16) if k % 3 == 1 else near_in[i, k].T


def at_an_end():
    place = lax.axis_index(AXES)
    return jnp.logical_or(place == 0, place == lax.axis_size(AXES) - 1)


def advance(step, last, image, field, scales, partial, matrices, outs):
    leaves = field.shape[0]
    root = scales[step * leaves : (step + 1) * leaves, :]
    after = field - image * root
    total = field * root
    if step:
        total += partial[...]
    if last:
        total += after * scales[(step + 1) * leaves : (step + 2) * leaves, :]
    else:
        outs[2][...] = after
    outs[0][...] = total
    write_stack(total if last else after, stacked(matrices[1]), stacked(matrices[3]), outs[1], matrices[5])


def image_of(field, own, mate, far, picks, matrices):
    near, leaf_basis, coupling, _, top, _, transfer_turned = matrices
    return apply_rows(
        field, own, mate, far, *picks, near, stacked(leaf_basis), coupling, transfer_turned, top
    )


def step_early(step, last, scales, product, partial, own, mate, *rest):
    picks, matrices, outs = rest[:3], rest[3:10], rest[10:]

    @pl.when(at_an_end())
    def _():
        field = product[...]
        image = image_of(field, own, mate, own, picks, matrices)
        advance(step, last, image, field, scales, partial, matrices, outs)


def step_late(step, last, scales, product, partial, own, mate, far, *rest):
    picks, matrices, rest = rest[:3], rest[3:10], rest[10:]
    ready, outs = rest[: len(rest) // 2], rest[len(rest) // 2 :]
    end = at_an_end()

    @pl.when(jnp.logical_not(end))
    def _():
        field = product[...]
        image = image_of(field, own, mate, far, picks, matrices)
        advance(step, last, image, field, scales, partial, matrices, outs)

    @pl.when(end)
    def _():
        for source, target in zip(ready, outs):
            target[...] = source[...]


def pack_iota(count):
    lane = lax.broadcasted_iota(jnp.int32, (count, 128), 1)
    return lane, lax.broadcasted_iota(jnp.int32, (count, 128), 0)


def last_early(field, own, mate, *rest):
    picks, matrices, (basis, image_out, gram) = rest[:3], rest[3:10], rest[10:]
    count = basis.shape[0]
    lane, sub = pack_iota(count)
    vectors = basis[...]
    packed = jnp.zeros((count, 128), F32)
    for n in range(count):
        column = jnp.sum(vectors * vectors[n : n + 1], axis=1, keepdims=True)
        packed = jnp.where(lane == n * count + sub, column, packed)
    gram[...] = packed

    @pl.when(at_an_end())
    def _():
        image_out[...] = image_of(field[...], own, mate, own, picks, matrices)


def last_late(field, own, mate, far, *rest):
    picks, matrices, (basis, ready, gram, image_out, sums) = rest[:3], rest[3:10], rest[10:]
    end = at_an_end()

    @pl.when(jnp.logical_not(end))
    def _():
        image_out[...] = image_of(field[...], own, mate, far, picks, matrices)

    @pl.when(end)
    def _():
        image_out[...] = ready[...]

    image = image_out[...]
    count, leaves = basis.shape[0], image.shape[0]
    lane, sub = pack_iota(count)
    packed = gram[...]
    dots = jnp.zeros((count, PANEL), F32)
    for i in range(leaves):
        dots += basis[:, i * PANEL : (i + 1) * PANEL] * image[i : i + 1]
    column = jnp.sum(dots, axis=1, keepdims=True)
    packed = jnp.where(lane == count * count + sub, column, packed)
    column = jnp.sum(image * image, axis=1, keepdims=True)
    packed = jnp.where(lane == count * count + count, column, packed)
    sums[...] = jnp.broadcast_to(jnp.sum(packed, axis=0, keepdims=True), sums.shape)


def finish_kernel(size, sums, image, basis, vector_out, hessen_out):
    count, leaves = basis.shape[0], image.shape[0]
    lane = lax.broadcasted_iota(jnp.int32, (count, 128), 1)
    sub = lax.broadcasted_iota(jnp.int32, (count, 128), 0)
    totals = jnp.broadcast_to(jnp.sum(sums[...], axis=0, keepdims=True) / size, (count, 128))
    zero = jnp.zeros((count, 128), F32)
    here = lane == count * count + sub
    coef = jnp.sum(jnp.where(here, totals, zero), axis=1, keepdims=True)
    inner = jnp.sum(jnp.where(lane % count == sub, coef, zero), axis=0, keepdims=True)
    outer = jnp.sum(jnp.where(lane // count == sub, coef, zero), axis=0, keepdims=True)
    gram = jnp.where(lane[:1] < count * count, totals[:1] * inner * outer, zero[:1])
    length = jnp.where(lane[:1] == count * count + count, totals[:1], zero[:1])
    squared = jnp.sum(gram + length, axis=1, keepdims=True)
    squared = squared - 2.0 * jnp.sum(coef * coef, axis=0, keepdims=True)
    beta = jnp.sqrt(squared + 1e-06)
    for i in range(leaves):
        taken = jnp.sum(coef * basis[:, i * PANEL : (i + 1) * PANEL], axis=0, keepdims=True)
        row = (image[i : i + 1, :] - taken) / beta
        vector_out[2 * i : 2 * i + 1, :] = row[:, : PANEL // 2]
        vector_out[2 * i + 1 : 2 * i + 2, :] = row[:, PANEL // 2 :]
    values = jnp.sum(jnp.where(lane == sub, coef, zero), axis=0, keepdims=True)
    hessen_out[...] = jnp.where(lane[:1] == count, beta, values)[0, : count + 1]


def call(kernel, specs, outs, scratch=()):
    shapes = [jax.ShapeDtypeStruct(shape, dtype) for shape, dtype in outs]
    return pl.pallas_call(
        kernel,
        out_shape=shapes,
        in_specs=specs,
        out_specs=[VMEM] * len(shapes),
        scratch_shapes=list(scratch),
        compiler_params=pltpu.CompilerParams(vmem_limit_bytes=24 << 20),
    )


def pinned(*arrays):
    return [pltpu.with_memory_space_constraint(a, pltpu.HBM) for a in arrays]


def like(array):
    return pltpu.VMEM(array.shape, array.dtype)


def body(
    basis, roots, near_blocks, near_ids, leaf_basis, far_coupling, far_ids, transfer, top_coupling, top_ids
):
    leaves, nears = near_blocks.shape[:2]
    fars, parents, tops = far_coupling.shape[1], *top_coupling.shape[:2]
    devices = lax.axis_size("grp") * lax.axis_size("leaf")
    mates = [(i, i ^ 1) for i in range(devices)]
    others = [(i, (((i + 1) ^ 1) - 1) % devices) for i in range(devices)]

    product, stack, basis, leaf_basis, transfer = call(
        start_kernel,
        [HBM] * 3,
        [((leaves, PANEL), F32), ((leaves, WIDTH), BF16)] + [(a.shape, a.dtype) for a in (basis, leaf_basis, transfer)],
        [pltpu.SemaphoreType.DMA((3,))],
    )(*pinned(basis, leaf_basis, transfer))
    far = lax.ppermute(stack, AXES, others)
    mate = lax.ppermute(stack, AXES, mates)
    mate, far = lax.optimization_barrier((mate, far))
    roots = roots.reshape(1, -1)
    scales, basis_turned, transfer_turned, near, coupling, top, *picks = call(
        prepare_kernel,
        [VMEM] * 3 + [HBM] * 7,
        [
            ((roots.shape[1] * leaves, PANEL), F32),
            ((PANEL, leaves * RANK), BF16),
            ((PRANK, leaves * RANK), BF16),
            (near_blocks.shape, BF16),
            ((fars * RANK, leaves * RANK), BF16),
            ((tops * PRANK, parents * PRANK), BF16),
            ((nears * leaves, SOURCES), BF16),
            ((fars * leaves, SOURCES), BF16),
            ((tops * leaves, SOURCES), BF16),
        ],
        [like(a) for a in (roots, near_blocks, far_coupling, top_coupling, near_ids, far_ids, top_ids)]
        + [pltpu.SemaphoreType.DMA((6 + leaves,))],
    )(product, leaf_basis, transfer, *pinned(roots, near_blocks, near_ids, far_coupling, far_ids, top_coupling, top_ids))
    matrices = (*picks, near, leaf_basis, coupling, transfer, top, basis_turned, transfer_turned)
    partial = product
    steps = roots.shape[1] - 1
    square = ((leaves, PANEL), F32)
    for step in range(steps):
        last = step == steps - 1
        outs = [square, ((leaves, WIDTH), BF16)] + ([] if last else [square])
        state = (scales, product, partial, stack, mate)
        ready = call(functools.partial(step_early, step, last), [VMEM] * 15, outs)(*state, *matrices)
        partial, stack, *after = call(
            functools.partial(step_late, step, last), [VMEM] * (16 + len(outs)), outs
        )(*state, far, *matrices, *ready)
        product = None if last else after[0]
        far = lax.ppermute(stack, AXES, others)
        mate = lax.ppermute(stack, AXES, mates)
    state = (partial, stack, mate)
    ready = call(last_early, [VMEM] * 14, [square, ((basis.shape[0], 128), F32)])(*state, *matrices, basis)
    image, sums = call(last_late, [VMEM] * 17, [square, ((devices, 128), F32)])(
        *state, far, *matrices, basis, *ready
    )
    sums = lax.all_to_all(sums.reshape(devices, 1, 128), AXES, 0, 0, tiled=True)
    size = float(leaves * PANEL * devices)
    vector, hessen = call(
        functools.partial(finish_kernel, size), [VMEM] * 3, [((leaves * 2, 128), F32), ((basis.shape[0] + 1,), F32)]
    )(sums.reshape(devices, 128), image, basis)
    return vector.reshape(leaves * PANEL), hessen


def solution(mesh):
    split = P(AXES)
    in_specs = (P(None, AXES), P()) + (split,) * 8
    return jax.shard_map(body, mesh=mesh, in_specs=in_specs, out_specs=(split, P()), check_vma=False)
```

```python
import functools

import jax
import jax.numpy as jnp
from jax import lax
from jax.experimental import pallas as pl
from jax.experimental.pallas import tpu as pltpu
from jax.sharding import PartitionSpec as P

AXES = ("grp", "leaf")
F32 = jnp.float32
BF16 = jnp.bfloat16
NT = (((1,), (1,)), ((), ()))
VMEM = pl.BlockSpec(memory_space=pltpu.VMEM)
HBM = pl.BlockSpec(memory_space=pltpu.HBM)
PANEL, RANK, PRANK, WIDTH = 256, 64, 128, 512
T_AT, C_AT = PANEL, PANEL + PRANK
SOURCES = 32


def dot(a, b):
    return jnp.dot(a, b, preferred_element_type=F32)


def dot_nt(a, b):
    return lax.dot_general(a, b, NT, preferred_element_type=F32)


def diagonal(value, block):
    lane = lax.broadcasted_iota(jnp.int32, value.shape, 1)
    row = lax.broadcasted_iota(jnp.int32, value.shape, 0)
    return jnp.where(lane // block == row, value, jnp.zeros_like(value))


def flat(value):
    return jnp.broadcast_to(jnp.sum(value, axis=0, keepdims=True), value.shape)


def write_stack(field, leaf_basis, transfer, stack, turned=None):
    rounded = field.astype(BF16)
    stack[:, :PANEL] = rounded
    coeffs = dot(rounded, turned[...]) if turned is not None else dot_nt(rounded, leaf_basis)
    kept = diagonal(coeffs, RANK)
    folded = sum(kept[:, at : at + 2 * RANK] for at in range(0, kept.shape[1], 2 * RANK))
    coeffs = folded[:, :RANK] + folded[:, RANK:]
    stack[:, C_AT:] = jnp.concatenate([coeffs, jnp.zeros_like(coeffs)], axis=1).astype(BF16)
    spread = diagonal(flat(kept.astype(BF16).astype(F32)), 2 * RANK)
    stack[:, T_AT:C_AT] = dot(spread.astype(BF16), transfer).astype(BF16)


def tiles(value, rows):
    return jnp.concatenate([value[at : at + rows] for at in range(0, value.shape[0], rows)], axis=1)


def apply_rows(field, own, mate, far, pick_near, pick_far, pick_top, near, leaf_basis, coupling, transfer_turned, top):
    leaves = field.shape[0]
    rest = jnp.zeros((SOURCES - 3 * leaves, WIDTH), F32)
    window = jnp.concatenate(
        [own[...].astype(F32), mate[...].astype(F32), far[...].astype(F32), rest], axis=0
    ).astype(BF16)
    panels = dot(pick_near[...], window[:, :PANEL]).astype(BF16)
    parents = tiles(dot(pick_top[...], window[:, T_AT:C_AT]), leaves).astype(BF16)
    coeffs = tiles(dot(pick_far[...], window[:, C_AT : C_AT + RANK]), leaves).astype(BF16)
    row = lax.broadcasted_iota(jnp.int32, field.shape, 0)

    def near_rows(total, some):
        for i in some:
            image = jnp.zeros(total.shape, F32)
            for k in range(near.shape[1]):
                image += dot(panels[k * leaves : (k + 1) * leaves], near[i, k])
            total += jnp.where(row == i, image, jnp.zeros_like(image))
        return total

    quarter = leaves // 4
    total = near_rows(0.5 * field, range(quarter))
    tops = diagonal(dot(parents, top[...]), PRANK)
    local = diagonal(dot(coeffs, coupling[...]), RANK)
    total = near_rows(total, range(quarter, 2 * quarter))
    tops = sum(tops[:, at : at + PRANK] for at in range(0, tops.shape[1], PRANK)).astype(BF16)
    local += diagonal(dot(tops, transfer_turned[...]), 2 * RANK)
    total = near_rows(total, range(2 * quarter, 3 * quarter))
    rows = dot(diagonal(flat(local), RANK).astype(BF16), leaf_basis)
    total = near_rows(total, range(3 * quarter, leaves))
    return total + rows


def stacked(ref):
    return ref[...].reshape(ref.shape[0] * ref.shape[1], ref.shape[2])


def start_kernel(basis, leaf_basis, transfer, product, stack, basis_in, leaf_basis_in, transfer_in, sems):
    copies = [
        pltpu.make_async_copy(source, target, sems.at[n])
        for n, (source, target) in enumerate(
            ((basis, basis_in), (leaf_basis, leaf_basis_in), (transfer, transfer_in))
        )
    ]
    for copy in copies:
        copy.start()
    copies[0].wait()
    count = basis.shape[0]
    for i in range(product.shape[0]):
        product[i : i + 1, :] = basis_in[count - 1 : count, i * PANEL : (i + 1) * PANEL]
    for copy in copies[1:]:
        copy.wait()
    write_stack(product[...], stacked(leaf_basis_in), stacked(transfer_in), stack)


def identity(size):
    row = lax.broadcasted_iota(jnp.int32, (size, size), 0)
    return jnp.where(row == lax.broadcasted_iota(jnp.int32, (size, size), 1), 1.0, 0.0).astype(BF16)


def prepare_kernel(
    _, leaf_basis, transfer, roots, near, near_ids, coupling, far_ids, top, top_ids,
    scales, basis_turned, transfer_turned, near_out, coupling_out, top_out, pick_near, pick_far, pick_top,
    roots_in, near_in, coupling_in, top_in, near_ids_in, far_ids_in, top_ids_in, sems,
):
    leaves = near.shape[0]
    pairs = [
        (roots, roots_in), (near_ids, near_ids_in), (far_ids, far_ids_in), (top_ids, top_ids_in),
        (coupling, coupling_in), (top, top_in),
    ] + [(near.at[i], near_in.at[i]) for i in range(leaves)]
    copies = [
        pltpu.make_async_copy(source, target, sems.at[n]) for n, (source, target) in enumerate(pairs)
    ]
    for copy in copies:
        copy.start()
    basis_turned[...] = stacked(leaf_basis).T
    transfer_turned[...] = stacked(transfer).T
    unit = identity(PANEL)
    for copy in copies[:6]:
        copy.wait()
    for k in range(roots.shape[1]):
        scales[k * leaves : (k + 1) * leaves, :] = jnp.broadcast_to(
            1.0 / roots_in[:, k : k + 1], (leaves, scales.shape[1])
        )
    place = lax.axis_index(AXES)
    odd = place % 2 == 1
    left, right = jnp.where(odd, leaves, 2 * leaves), jnp.where(odd, 2 * leaves, leaves)
    for ids_in, pick, rows in (
        (near_ids_in, pick_near, leaves), (far_ids_in, pick_far, leaves), (top_ids_in, pick_top, leaves // 2),
    ):
        away = ids_in[...] - place * rows
        where = jnp.where(away < 0, away + rows + left, jnp.where(away < rows, away, away - rows + right))
        lane = lax.broadcasted_iota(jnp.int32, (rows, SOURCES), 1)
        for k in range(ids_in.shape[1]):
            hot = jnp.where(lane == where[:, k : k + 1], 1.0, 0.0)
            if rows < leaves:
                hot = jnp.concatenate([hot, jnp.zeros((leaves - rows, SOURCES), F32)], axis=0)
            pick[k * leaves : (k + 1) * leaves, :] = hot.astype(BF16)
    for k in range(coupling.shape[1]):
        rows = jnp.concatenate([coupling_in[i, k] for i in range(leaves)], axis=0)
        coupling_out[k * RANK : (k + 1) * RANK, :] = rows.T
    for p in range(top.shape[0]):
        for k in range(top.shape[1]):
            rows, lanes = slice(k * PRANK, (k + 1) * PRANK), slice(p * PRANK, (p + 1) * PRANK)
            top_out[rows, lanes] = top_in[p, k].T
    for i in range(leaves):
        for copy in copies[6 + i : 8 + i] if i % 2 == 0 else ():
            copy.wait()
        for k in range(near.shape[1]):
            near_out[i, k] = dot_nt(unit, near_in[i, k]).astype(BF16) if k % 3 == 1 else near_in[i, k].T


def at_an_end():
    place = lax.axis_index(AXES)
    return jnp.logical_or(place == 0, place == lax.axis_size(AXES) - 1)


def advance(step, last, image, field, scales, partial, matrices, outs):
    leaves = field.shape[0]
    root = scales[step * leaves : (step + 1) * leaves, :]
    after = field - image * root
    total = field * root
    if step:
        total += partial[...]
    if last:
        total += after * scales[(step + 1) * leaves : (step + 2) * leaves, :]
    else:
        outs[2][...] = after
    outs[0][...] = total
    write_stack(total if last else after, stacked(matrices[1]), stacked(matrices[3]), outs[1], matrices[5])


def image_of(field, own, mate, far, picks, matrices):
    near, leaf_basis, coupling, _, top, _, transfer_turned = matrices
    return apply_rows(
        field, own, mate, far, *picks, near, stacked(leaf_basis), coupling, transfer_turned, top
    )


def step_early(step, last, scales, product, partial, own, mate, *rest):
    picks, matrices, outs = rest[:3], rest[3:10], rest[10:]

    @pl.when(at_an_end())
    def _():
        field = product[...]
        image = image_of(field, own, mate, own, picks, matrices)
        advance(step, last, image, field, scales, partial, matrices, outs)


def step_late(step, last, scales, product, partial, own, mate, far, *rest):
    picks, matrices, rest = rest[:3], rest[3:10], rest[10:]
    ready, outs = rest[: len(rest) // 2], rest[len(rest) // 2 :]
    end = at_an_end()

    @pl.when(jnp.logical_not(end))
    def _():
        field = product[...]
        image = image_of(field, own, mate, far, picks, matrices)
        advance(step, last, image, field, scales, partial, matrices, outs)

    @pl.when(end)
    def _():
        for source, target in zip(ready, outs):
            target[...] = source[...]


def pack_iota(count):
    lane = lax.broadcasted_iota(jnp.int32, (count, 128), 1)
    return lane, lax.broadcasted_iota(jnp.int32, (count, 128), 0)


def last_early(field, own, mate, *rest):
    picks, matrices, (basis, image_out, gram) = rest[:3], rest[3:10], rest[10:]
    count = basis.shape[0]
    lane, sub = pack_iota(count)
    vectors = basis[...]
    packed = jnp.zeros((count, 128), F32)
    for n in range(count):
        column = jnp.sum(vectors * vectors[n : n + 1], axis=1, keepdims=True)
        packed = jnp.where(lane == n * count + sub, column, packed)
    gram[...] = packed

    @pl.when(at_an_end())
    def _():
        image_out[...] = image_of(field[...], own, mate, own, picks, matrices)


def last_late(field, own, mate, far, *rest):
    picks, matrices, (basis, ready, gram, image_out, sums) = rest[:3], rest[3:10], rest[10:]
    end = at_an_end()

    @pl.when(jnp.logical_not(end))
    def _():
        image_out[...] = image_of(field[...], own, mate, far, picks, matrices)

    @pl.when(end)
    def _():
        image_out[...] = ready[...]

    image = image_out[...]
    count, leaves = basis.shape[0], image.shape[0]
    lane, sub = pack_iota(count)
    packed = gram[...]
    dots = jnp.zeros((count, PANEL), F32)
    for i in range(leaves):
        dots += basis[:, i * PANEL : (i + 1) * PANEL] * image[i : i + 1]
    column = jnp.sum(dots, axis=1, keepdims=True)
    packed = jnp.where(lane == count * count + sub, column, packed)
    column = jnp.sum(image * image, axis=1, keepdims=True)
    packed = jnp.where(lane == count * count + count, column, packed)
    sums[...] = jnp.broadcast_to(jnp.sum(packed, axis=0, keepdims=True), sums.shape)


def finish_kernel(size, sums, image, basis, vector_out, hessen_out):
    count, leaves = basis.shape[0], image.shape[0]
    lane = lax.broadcasted_iota(jnp.int32, (count, 128), 1)
    sub = lax.broadcasted_iota(jnp.int32, (count, 128), 0)
    totals = jnp.broadcast_to(jnp.sum(sums[...], axis=0, keepdims=True) / size, (count, 128))
    zero = jnp.zeros((count, 128), F32)
    here = lane == count * count + sub
    coef = jnp.sum(jnp.where(here, totals, zero), axis=1, keepdims=True)
    inner = jnp.sum(jnp.where(lane % count == sub, coef, zero), axis=0, keepdims=True)
    outer = jnp.sum(jnp.where(lane // count == sub, coef, zero), axis=0, keepdims=True)
    gram = jnp.where(lane[:1] < count * count, totals[:1] * inner * outer, zero[:1])
    length = jnp.where(lane[:1] == count * count + count, totals[:1], zero[:1])
    squared = jnp.sum(gram + length, axis=1, keepdims=True)
    squared = squared - 2.0 * jnp.sum(coef * coef, axis=0, keepdims=True)
    beta = jnp.sqrt(squared + 1e-06)
    for i in range(leaves):
        taken = jnp.sum(coef * basis[:, i * PANEL : (i + 1) * PANEL], axis=0, keepdims=True)
        row = (image[i : i + 1, :] - taken) / beta
        vector_out[2 * i : 2 * i + 1, :] = row[:, : PANEL // 2]
        vector_out[2 * i + 1 : 2 * i + 2, :] = row[:, PANEL // 2 :]
    values = jnp.sum(jnp.where(lane == sub, coef, zero), axis=0, keepdims=True)
    hessen_out[...] = jnp.where(lane[:1] == count, beta, values)[0, : count + 1]


def call(kernel, specs, outs, scratch=()):
    shapes = [jax.ShapeDtypeStruct(shape, dtype) for shape, dtype in outs]
    return pl.pallas_call(
        kernel,
        out_shape=shapes,
        in_specs=specs,
        out_specs=[VMEM] * len(shapes),
        scratch_shapes=list(scratch),
        compiler_params=pltpu.CompilerParams(vmem_limit_bytes=24 << 20),
    )


def pinned(*arrays):
    return [pltpu.with_memory_space_constraint(a, pltpu.HBM) for a in arrays]


def like(array):
    return pltpu.VMEM(array.shape, array.dtype)


def body(
    basis, roots, near_blocks, near_ids, leaf_basis, far_coupling, far_ids, transfer, top_coupling, top_ids
):
    leaves, nears = near_blocks.shape[:2]
    fars, parents, tops = far_coupling.shape[1], *top_coupling.shape[:2]
    devices = lax.axis_size("grp") * lax.axis_size("leaf")
    mates = [(i, i ^ 1) for i in range(devices)]
    others = [(i, (((i + 1) ^ 1) - 1) % devices) for i in range(devices)]

    product, stack, basis, leaf_basis, transfer = call(
        start_kernel,
        [HBM] * 3,
        [((leaves, PANEL), F32), ((leaves, WIDTH), BF16)] + [(a.shape, a.dtype) for a in (basis, leaf_basis, transfer)],
        [pltpu.SemaphoreType.DMA((3,))],
    )(*pinned(basis, leaf_basis, transfer))
    far = lax.ppermute(stack, AXES, others)
    mate = lax.ppermute(stack, AXES, mates)
    mate, far = lax.optimization_barrier((mate, far))
    roots = roots.reshape(1, -1)
    scales, basis_turned, transfer_turned, near, coupling, top, *picks = call(
        prepare_kernel,
        [VMEM] * 3 + [HBM] * 7,
        [
            ((roots.shape[1] * leaves, PANEL), F32),
            ((PANEL, leaves * RANK), BF16),
            ((PRANK, leaves * RANK), BF16),
            (near_blocks.shape, BF16),
            ((fars * RANK, leaves * RANK), BF16),
            ((tops * PRANK, parents * PRANK), BF16),
            ((nears * leaves, SOURCES), BF16),
            ((fars * leaves, SOURCES), BF16),
            ((tops * leaves, SOURCES), BF16),
        ],
        [like(a) for a in (roots, near_blocks, far_coupling, top_coupling, near_ids, far_ids, top_ids)]
        + [pltpu.SemaphoreType.DMA((6 + leaves,))],
    )(product, leaf_basis, transfer, *pinned(roots, near_blocks, near_ids, far_coupling, far_ids, top_coupling, top_ids))
    matrices = (*picks, near, leaf_basis, coupling, transfer, top, basis_turned, transfer_turned)
    partial = product
    steps = roots.shape[1] - 1
    square = ((leaves, PANEL), F32)
    for step in range(steps):
        last = step == steps - 1
        outs = [square, ((leaves, WIDTH), BF16)] + ([] if last else [square])
        state = (scales, product, partial, stack, mate)
        ready = call(functools.partial(step_early, step, last), [VMEM] * 15, outs)(*state, *matrices)
        partial, stack, *after = call(
            functools.partial(step_late, step, last), [VMEM] * (16 + len(outs)), outs
        )(*state, far, *matrices, *ready)
        product = None if last else after[0]
        far = lax.ppermute(stack, AXES, others)
        mate = lax.ppermute(stack, AXES, mates)
    state = (partial, stack, mate)
    ready = call(last_early, [VMEM] * 14, [square, ((basis.shape[0], 128), F32)])(*state, *matrices, basis)
    image, sums = call(last_late, [VMEM] * 17, [square, ((devices, 128), F32)])(
        *state, far, *matrices, basis, *ready
    )
    sums = lax.all_to_all(sums.reshape(devices, 1, 128), AXES, 0, 0, tiled=True)
    size = float(leaves * PANEL * devices)
    vector, hessen = call(
        functools.partial(finish_kernel, size), [VMEM] * 3, [((leaves * 2, 128), F32), ((basis.shape[0] + 1,), F32)]
    )(sums.reshape(devices, 128), image, basis)
    return vector.reshape(leaves * PANEL), hessen


def solution(mesh):
    split = P(AXES)
    in_specs = (P(None, AXES), P()) + (split,) * 8
    return jax.shard_map(body, mesh=mesh, in_specs=in_specs, out_specs=(split, P()), check_vma=False)
```
